32 devices in a mesh: lat: 4 (over y, x), lon: 8 (over z, core).
Axes of the slice: x: 2, y: 2, z: 4, core: 2. Of those that a mesh axis runs over, the one named last changes fastest.
Arguments:
- coarse_field: bfloat16 [1, 128, 128, 512], P(None, None, 'lat', 'lon'), may hold values from -6 to 6
- cotangent: bfloat16 [1, 64, 256, 1024], P(None, None, 'lat', 'lon'), may hold values from -6 to 6
- tconv_weight: bfloat16 [4, 64, 128], replicated, may hold values from -0.5 to 0.5
- conv_weight: bfloat16 [64, 576], replicated, may hold values from -0.25 to 0.25
Outputs:
- coarse_grad: bfloat16 [1, 128, 128, 512], P(None, None, 'lat', 'lon')
- tconv_grad: float32 [4, 64, 128], replicated
- conv_grad: float32 [64, 576], replicated
The draws below stay inside these ranges and needn't reach their ends.
All inputs are finite; a program needn't handle non-finite values.
Results may differ from the reference program's by a relative error of at most 0.0049.
Values may be sent and summed in bfloat16 or wider, within the bound.
No kernel may reach another device: no remote copies, remote signals or barrier semaphores. Data moves between devices by JAX's collectives and lax.ppermute only.
A program may use at most 128 MiB of HBM per device.

```python
import math
import jax
import jax.numpy as jnp
from jax import lax

C_IN = 128
C2 = 64
NB = 1
NLAT = 256
NLON = 1024
HLAT = 128
HLON = 512


def block_scale(own_key, shape, split, least, largest):
    gain, own = 1.0, jax.random.fold_in(own_key, 6)
    for position, shards_of in split:
        draws = jnp.exp(jax.random.uniform(jax.random.fold_in(own, position), (shards_of,), jnp.float32, least / len(split), largest / len(split)))
        gain = gain * jnp.repeat(draws, shape[position] // shards_of).reshape([-1 if axis == position else 1 for axis in range(len(shape))])
    return gain


def scatter_about(key, extent, deviation, reach, shards=(), kind=jnp.bfloat16):
    values = jax.random.normal(key, extent, jnp.float32) * deviation
    if len(shards) > 0:
        values = block_scale(key, extent, shards, -0.22, 0.18) * values
    return jnp.clip(values, min=-reach, max=reach).astype(kind)


def setup_inputs(seed: int = 0) -> dict:
    streams_of = jax.random.split(jax.random.key(seed), 5)
    coarse_field = scatter_about(streams_of[0], (NB, C_IN, HLAT, HLON), 1.0, 6.0, ((2, 4), (3, 8)))
    cotangent = scatter_about(streams_of[1], (NB, C2, NLAT, NLON), 1.0, 6.0, ((2, 4), (3, 8)))
    tconv_weight = scatter_about(streams_of[2], (4, C2, C_IN), C_IN ** -0.5, 0.5)
    conv_weight = scatter_about(streams_of[3], (C2, 9 * C2), (9 * C2) ** -0.5, 0.25)
    return dict(coarse_field=coarse_field, cotangent=cotangent, tconv_weight=tconv_weight, conv_weight=conv_weight)


OFFSETS = ((-1, -1), (-1, 0), (-1, 1), (0, -1), (0, 0), (0, 1), (1, -1), (1, 0), (1, 1))

def silu_slope(values):
    logistic = jax.nn.sigmoid(values)
    return logistic * (1.0 + values * (1.0 - logistic))

def extend_globe(field):
    opposite = field.shape[2] // 2
    top_row = jnp.roll(field[:, :1, :], -opposite, axis=2)
    bottom_row = jnp.roll(field[:, -1:, :], -opposite, axis=2)
    rows = jnp.concatenate([top_row, field, bottom_row], axis=1)
    return jnp.concatenate([rows[:, :, -1:], rows, rows[:, :, :1]], axis=2)

def reference(coarse_field, cotangent, tconv_weight, conv_weight):
    channels = conv_weight.shape[0]
    in_channels = tconv_weight.shape[2]
    rows_all = coarse_field.shape[2] * 2
    cols_all = coarse_field.shape[3] * 2
    scale = 1.0 / math.sqrt(coarse_field.shape[0] * rows_all * cols_all)
    tconv_taps = tconv_weight.astype(jnp.float32).reshape(2, 2, channels, in_channels)
    conv_taps = conv_weight.astype(jnp.float32).reshape(channels, 9, channels)

    def one_sample(carry, pair):
        coarse, grad_out = pair
        coarse32 = coarse.astype(jnp.float32)
        upsampled = jnp.einsum('pqck,kij->cipjq', tconv_taps, coarse32).reshape(channels, rows_all, cols_all)
        activated = (upsampled * jax.nn.sigmoid(upsampled)).astype(jnp.bfloat16)
        extended = extend_globe(activated).astype(jnp.float32)
        grad32 = grad_out.astype(jnp.float32)
        conv_terms = []
        scattered = jnp.zeros((channels, rows_all + 2, cols_all + 2), jnp.float32)
        for tap_index, (row_step, col_step) in enumerate(OFFSETS):
            window = extended[:, 1 + row_step:1 + row_step + rows_all, 1 + col_step:1 + col_step + cols_all]
            conv_terms.append(jnp.einsum('ors,crs->oc', grad32, window))
            part = jnp.einsum('oc,ors->crs', conv_taps[:, tap_index], grad32)
            scattered = scattered + jnp.pad(part, ((0, 0), (1 + row_step, 1 - row_step), (1 + col_step, 1 - col_step)))
        inner = scattered[:, :, 1:-1]
        inner = inner.at[:, :, -1].add(scattered[:, :, 0])
        inner = inner.at[:, :, 0].add(scattered[:, :, -1])
        opposite = cols_all // 2
        feature_grad = inner[:, 1:-1]
        feature_grad = feature_grad.at[:, 0].add(jnp.roll(inner[:, 0], opposite, axis=1))
        feature_grad = feature_grad.at[:, -1].add(jnp.roll(inner[:, -1], opposite, axis=1))
        pre_grad = (feature_grad * silu_slope(upsampled)).astype(jnp.bfloat16)
        blocks = pre_grad.astype(jnp.float32).reshape(channels, rows_all // 2, 2, cols_all // 2, 2)
        coarse_grad = jnp.einsum('pqck,cipjq->kij', tconv_taps, blocks).astype(jnp.bfloat16)
        tap_grad = jnp.einsum('cipjq,kij->pqck', blocks, coarse32).reshape(4, channels, in_channels)
        conv_sum = jnp.stack(conv_terms, axis=1).reshape(channels, 9 * channels)
        return ((carry[0] + tap_grad, carry[1] + conv_sum), coarse_grad)
    start = (jnp.zeros((4, channels, in_channels), jnp.float32), jnp.zeros((channels, 9 * channels), jnp.float32))
    totals, coarse_grads = lax.scan(one_sample, start, (coarse_field, cotangent))
    return (coarse_grads, totals[0] * scale, totals[1] * scale)
```

```python
import math

import jax
import jax.numpy as jnp
from jax import lax
from jax.sharding import PartitionSpec as P

OFFSETS = ((-1, -1), (-1, 0), (-1, 1), (0, -1), (0, 0), (0, 1), (1, -1), (1, 0), (1, 1))


def shifted(array, axis, by):
    length = lax.axis_size(axis)
    return lax.ppermute(array, axis, [(i, (i + by) % length) for i in range(length)])


def with_halo(cells, sides, width, closed):
    for axis, dim in sides:
        count = lax.axis_size(axis)
        ends = count if closed else count - 1
        head = lax.slice_in_dim(cells, 0, width, axis=dim)
        tail = lax.slice_in_dim(cells, cells.shape[dim] - width, cells.shape[dim], axis=dim)
        cells = jnp.concatenate(
            [
                lax.ppermute(tail, axis, [(i, (i + 1) % count) for i in range(ends)]),
                cells,
                lax.ppermute(head, axis, [((i + 1) % count, i) for i in range(ends)]),
            ],
            axis=dim,
        )
    return cells


def silu_slope(values):
    logistic = jax.nn.sigmoid(values)
    return logistic * (1.0 + values * (1.0 - logistic))


def fix_poles(padded):
    lat_pos = lax.axis_index("lat")
    last_band = lax.axis_size("lat") - 1
    opposite = lax.axis_size("lon") // 2
    inner_rows = padded.shape[2] - 2
    at_north = lat_pos == 0
    outgoing = jnp.where(at_north, padded[:, :, 1], padded[:, :, inner_rows])
    incoming = shifted(outgoing, "lon", opposite)
    top_row = jnp.where(at_north, incoming, padded[:, :, 0])
    bottom_row = jnp.where(lat_pos == last_band, incoming, padded[:, :, inner_rows + 1])
    return jnp.concatenate(
        [top_row[:, :, None], padded[:, :, 1 : inner_rows + 1], bottom_row[:, :, None]], axis=2
    )


def extend(field):
    padded = with_halo(field, (("lat", 2),), 1, False)
    padded = fix_poles(padded)
    return with_halo(padded, (("lon", 3),), 1, True)


def cotangent_rims(cotangent, conv_taps):
    lat_pos = lax.axis_index("lat")
    last_band = lax.axis_size("lat") - 1
    rows_here = cotangent.shape[2]
    cols_here = cotangent.shape[3]
    extended = extend(cotangent)
    total = None
    for tap_index, (row_step, col_step) in enumerate(OFFSETS):
        window = extended[
            :, :, 1 - row_step : 1 - row_step + rows_here, 1 - col_step : 1 - col_step + cols_here
        ]
        term = jnp.einsum(
            "oc,nors->ncrs", conv_taps[:, tap_index], window, preferred_element_type=jnp.float32
        )
        total = term if total is None else total + term
    north_fix = None
    south_fix = None
    for col_step in (-1, 0, 1):
        upper_tap = col_step + 1
        lower_tap = 7 + col_step
        top_cells = extended[:, :, 0, 1 - col_step : 1 - col_step + cols_here]
        bottom_cells = extended[:, :, rows_here + 1, 1 - col_step : 1 - col_step + cols_here]
        upper_top = jnp.einsum(
            "oc,nos->ncs", conv_taps[:, upper_tap], top_cells, preferred_element_type=jnp.float32
        )
        lower_top = jnp.einsum(
            "oc,nos->ncs", conv_taps[:, lower_tap], top_cells, preferred_element_type=jnp.float32
        )
        upper_bottom = jnp.einsum(
            "oc,nos->ncs", conv_taps[:, upper_tap], bottom_cells, preferred_element_type=jnp.float32
        )
        lower_bottom = jnp.einsum(
            "oc,nos->ncs", conv_taps[:, lower_tap], bottom_cells, preferred_element_type=jnp.float32
        )
        north_term = upper_top - lower_top
        south_term = lower_bottom - upper_bottom
        north_fix = north_term if north_fix is None else north_fix + north_term
        south_fix = south_term if south_fix is None else south_fix + south_term
    first_row = total[:, :, 0] + jnp.where(lat_pos == 0, north_fix, 0.0)
    final_row = total[:, :, -1] + jnp.where(lat_pos == last_band, south_fix, 0.0)
    return jnp.concatenate(
        [first_row[:, :, None], total[:, :, 1:-1], final_row[:, :, None]], axis=2
    )


def summed_everywhere(arrays, axes, scale):
    members = lax.axis_size(axes)
    flat = jnp.concatenate([array.reshape(-1) for array in arrays])
    piece = -(-flat.shape[0] // (members * 128)) * 128
    flat = jnp.pad(flat, (0, members * piece - flat.shape[0]))
    parts = lax.all_to_all(flat.reshape(members, piece), axes, 0, 0, tiled=True)
    own = jnp.sum(parts, axis=0) * scale
    spread = jnp.broadcast_to(own[None], (members, piece))
    whole = lax.all_to_all(spread, axes, 0, 0, tiled=True).reshape(-1)
    outs, start = [], 0
    for array in arrays:
        outs.append(whole[start : start + array.size].reshape(array.shape))
        start += array.size
    return outs


def per_device(coarse_field, cotangent, tconv_weight, conv_weight):
    batch, channels, rows_here, cols_here = cotangent.shape
    in_channels = coarse_field.shape[1]
    tconv_taps = tconv_weight.reshape(2, 2, channels, in_channels)
    conv_taps = conv_weight.reshape(channels, 9, channels)
    upsampled = jnp.einsum(
        "pqck,nkij->ncipjq", tconv_taps, coarse_field, preferred_element_type=jnp.float32
    )
    upsampled = upsampled.reshape(batch, channels, rows_here, cols_here)
    activated = (upsampled * jax.nn.sigmoid(upsampled)).astype(jnp.bfloat16)
    extended = extend(activated)
    conv_terms = []
    for tap_index, (row_step, col_step) in enumerate(OFFSETS):
        window = extended[
            :, :, 1 + row_step : 1 + row_step + rows_here, 1 + col_step : 1 + col_step + cols_here
        ]
        conv_terms.append(
            jnp.einsum("nors,ncrs->oc", cotangent, window, preferred_element_type=jnp.float32)
        )
    conv_grad = jnp.stack(conv_terms, axis=1).reshape(channels, 9 * channels)
    feature_grad = cotangent_rims(cotangent, conv_taps)
    pre_grad = (feature_grad * silu_slope(upsampled)).astype(jnp.bfloat16)
    pre_blocks = pre_grad.reshape(batch, channels, rows_here // 2, 2, cols_here // 2, 2)
    coarse_grad = jnp.einsum(
        "pqck,ncipjq->nkij", tconv_taps, pre_blocks, preferred_element_type=jnp.float32
    ).astype(jnp.bfloat16)
    tconv_grad = jnp.einsum(
        "ncipjq,nkij->pqck", pre_blocks, coarse_field, preferred_element_type=jnp.float32
    )
    tconv_grad = tconv_grad.reshape(4, channels, in_channels)
    total_cells = batch * rows_here * cols_here * lax.axis_size("lat") * lax.axis_size("lon")
    scale = 1.0 / math.sqrt(total_cells)
    tconv_grad, conv_grad = summed_everywhere((tconv_grad, conv_grad), ("lat", "lon"), scale)
    return (coarse_grad, tconv_grad, conv_grad)


def solution(mesh):
    return jax.shard_map(
        per_device,
        mesh=mesh,
        in_specs=(P(None, None, "lat", "lon"), P(None, None, "lat", "lon"), P(), P()),
        out_specs=(P(None, None, "lat", "lon"), P(), P()),
        check_vma=False,
    )
```

```python
import functools
import math

import jax
import jax.numpy as jnp
from jax import lax
from jax.experimental import pallas as pl
from jax.experimental.pallas import tpu as pltpu
from jax.sharding import PartitionSpec as P

F32, BF16 = jnp.float32, jnp.bfloat16
AXES = ("lat", "lon")
SHIFTS = (-1, 0, 1, 2)
VMEM = pl.BlockSpec(memory_space=pltpu.VMEM)
SMEM = pl.BlockSpec(memory_space=pltpu.SMEM)


def product(lhs, rhs, lhs_dim, rhs_dim):
    dims = (((lhs_dim,), (rhs_dim,)), ((), ()))
    return lax.dot_general(lhs, rhs, dims, preferred_element_type=F32)


def gather_kernel(flags, cot, recv_a, recv_b, near, send_a, send_b, wide, edges):
    channels, rows, cols = cot.shape
    half = cols // 2
    pairs = near.shape[0]
    north_is_a = flags[0] == 1

    def widen(o, carry):
        start = pl.multiple_of(o * rows, rows)
        wide[pl.ds(start, rows), :] = cot[o].astype(F32)
        return carry

    lax.fori_loop(0, channels, widen, 0, unroll=4)
    row_id = lax.broadcasted_iota(jnp.int32, (4 * half, cols), 0)
    col_id = lax.broadcasted_iota(jnp.int32, (4 * half, cols), 1)
    shift = row_id // half - 1
    pick = jnp.where(col_id == 2 * (row_id % half) + shift, 1.0, 0.0).astype(BF16)
    from_a = recv_a[...].astype(F32)
    from_b = recv_b[...].astype(F32)
    top = jnp.where(north_is_a, from_a, from_b).astype(BF16)
    bottom = jnp.where(north_is_a, from_b, from_a).astype(BF16)

    def row(r):
        return wide[pl.ds(r, channels, stride=rows), :].astype(BF16)

    def emit(m, parts):
        out = product(pick, jnp.concatenate(parts, axis=0), 1, 1)
        for k in range(len(parts) // 2):
            block = out[:, k * 2 * channels : (k + 1) * 2 * channels]
            near[m + k] = block.astype(BF16)
            edges[0, pl.ds(m + k, 1), :] = block[half : half + 1]
            edges[1, pl.ds(m + k, 1), :] = block[3 * half - 1 : 3 * half]

    emit(0, [top, row(0)])

    def middle(q, carry):
        m = 1 + 2 * q
        emit(m, [row(2 * m - 1), row(2 * m), row(2 * m + 1), row(2 * m + 2)])
        return carry

    lax.fori_loop(0, (pairs - 3) // 2, middle, 0)
    emit(pairs - 2, [row(rows - 3), row(rows - 2), row(rows - 1), bottom])
    odd = flags[1] == 1
    send_a[...] = jnp.where(odd, edges[0], edges[1]).astype(BF16)
    send_b[...] = jnp.where(odd, edges[1], edges[0]).astype(BF16)


def main_kernel(flags, x, near_in, recv_a, recv_b, up_w, conv_w, grad, sums,
                near, polar, rims, weights, conv_acc, up_acc, feature, sem):
    channels = conv_w.shape[0]
    pairs, quad, lanes = near.shape
    half = quad // 4
    rows = pairs - 1
    group = 4
    cells = group * half
    steps = rows // group
    load = pltpu.make_async_copy(near_in, near, sem)
    load.start()
    weights[...] = jnp.zeros_like(weights)
    for d in range(4):
        for e in range(4):
            for p in range(2):
                for q in range(2):
                    a, b = p - SHIFTS[e], q - SHIFTS[d]
                    if abs(a) <= 1 and abs(b) <= 1:
                        tap = 3 * (a + 1) + b + 1
                        weights[
                            d,
                            e * channels : (e + 1) * channels,
                            (2 * p + q) * channels : (2 * p + q + 1) * channels,
                        ] = conv_w[:, tap * channels : (tap + 1) * channels]
    conv_acc[...] = jnp.zeros_like(conv_acc)
    up_acc[...] = jnp.zeros_like(up_acc)
    odd = flags[1] == 1
    from_a = recv_a[...].astype(F32)
    from_b = recv_b[...].astype(F32)
    rims[0] = jnp.where(odd, from_a, from_b)
    rims[1] = jnp.where(odd, from_b, from_a)
    load.wait()
    tile = 16
    tile_row = lax.broadcasted_iota(jnp.int32, (tile, lanes), 0)

    def set_rims(m, carry):
        west = near[m, 0:tile, :].astype(F32)
        near[m, 0:tile, :] = jnp.where(
            tile_row == 0, rims[0, pl.ds(m, 1), :], west
        ).astype(BF16)
        east = near[m, quad - tile : quad, :].astype(F32)
        near[m, quad - tile : quad, :] = jnp.where(
            tile_row == tile - 1, rims[1, pl.ds(m, 1), :], east
        ).astype(BF16)
        return carry

    lax.fori_loop(0, pairs, set_rims, 0, unroll=3)
    lane_id = lax.broadcasted_iota(jnp.int32, (quad, lanes), 1)
    at_north = flags[2] == 1
    at_south = flags[3] == 1

    @pl.when(at_north)
    def _():
        block = near[0].astype(F32)
        polar[0] = jnp.where(lane_id < channels, block, 0.0).astype(BF16)
        near[0] = jnp.where(lane_id < channels, 0.0, block).astype(BF16)

    @pl.when(at_south)
    def _():
        block = near[pairs - 1].astype(F32)
        polar[1] = jnp.where(lane_id < channels, 0.0, block).astype(BF16)
        near[pairs - 1] = jnp.where(lane_id < channels, block, 0.0).astype(BF16)

    def step(s, carry):
        first = s * group
        start = pl.multiple_of(s * cells, cells)
        coarse = x[pl.ds(start, cells), :]
        up = product(coarse, up_w[...], 1, 1)
        gate = 1.0 / (1.0 + jnp.exp(-up))
        active = (up * gate).astype(BF16)
        slope = gate * (1.0 + up * (1.0 - gate))
        active_t = active.T
        total = None
        for d in range(4):
            lower = near[pl.ds(first, group), d * half : (d + 1) * half, :]
            upper = near[pl.ds(first + 1, group), d * half : (d + 1) * half, :]
            around = jnp.concatenate(
                [lower.reshape(cells, lanes), upper.reshape(cells, lanes)], axis=1
            )
            term = product(around, weights[d], 1, 0)
            total = term if total is None else total + term
            conv_acc[d] += product(active_t, around, 1, 0)
        feature[...] = total

        @pl.when(jnp.logical_and(s == 0, at_north))
        def _():
            for d in range(4):
                cap = polar[0, d * half : (d + 1) * half, :]
                feature[0:half, 0:lanes] += product(cap, weights[d, lanes : 2 * lanes, 0:lanes], 1, 0)
                conv_acc[d, 0:lanes, lanes : 2 * lanes] += product(
                    active[0:half, 0:lanes], cap, 0, 0
                )

        @pl.when(jnp.logical_and(s == steps - 1, at_south))
        def _():
            for d in range(4):
                cap = polar[1, d * half : (d + 1) * half, :]
                feature[cells - half : cells, lanes : 2 * lanes] += product(
                    cap, weights[d, 0:lanes, lanes : 2 * lanes], 1, 0
                )
                conv_acc[d, lanes : 2 * lanes, 0:lanes] += product(
                    active[cells - half : cells, lanes : 2 * lanes], cap, 0, 0
                )

        pre = (feature[...] * slope).astype(BF16)
        grad[pl.ds(start, cells), :] = product(pre, up_w[...], 1, 0).astype(BF16)
        up_acc[...] += product(pre, coarse, 0, 0)
        return carry

    lax.fori_loop(0, steps, step, 0)
    fine = up_acc.shape[0]
    sums[0:fine, :] = up_acc[...]
    zero = jnp.zeros((channels, channels), F32)

    def tap_sum(tap):
        if tap > 8:
            return zero
        a, b = tap // 3 - 1, tap % 3 - 1
        total = None
        for p in range(2):
            for q in range(2):
                e, d = p - a + 1, q - b + 1
                part = conv_acc[
                    d,
                    (2 * p + q) * channels : (2 * p + q + 1) * channels,
                    e * channels : (e + 1) * channels,
                ]
                total = part if total is None else total + part
        return total

    for u in range(5):
        for k in range(2):
            feature[k * channels : (k + 1) * channels, 0:channels] = tap_sum(2 * u + k)
        block = feature[0 : 2 * channels, 0 : 2 * channels].T
        sums[fine + u * channels : fine + (u + 1) * channels, :] = block[0:channels]


def summed_everywhere(part, scale):
    members = lax.axis_size(AXES)
    rows, lanes = part.shape
    piece = -(-rows // members)
    if members * piece > rows:
        part = jnp.pad(part, ((0, members * piece - rows), (0, 0)))
    parts = lax.all_to_all(part.reshape(members, piece * lanes), AXES, 0, 0, tiled=True)
    own = jnp.sum(parts, axis=0) * scale
    spread = jnp.broadcast_to(own[None], (members, piece * lanes))
    whole = lax.all_to_all(spread, AXES, 0, 0, tiled=True)
    return whole.reshape(members * piece, lanes)[:rows]


def row_routes(lats, lons):
    half = lons // 2
    there = []
    for lat in range(lats):
        for lon in range(lons):
            if lon < half:
                target = (lat + 1, lon) if lat + 1 < lats else (lat, lon + half)
            else:
                target = (lat - 1, lon) if lat > 0 else (lat, lon - half)
            there.append((lat * lons + lon, target[0] * lons + target[1]))
    return there, [(b, a) for a, b in there]


def per_device(coarse_field, cotangent, tconv_weight, conv_weight):
    batch, channels, rows, cols = cotangent.shape
    in_channels = coarse_field.shape[1]
    lats, lons = lax.axis_size("lat"), lax.axis_size("lon")
    lat, lon = lax.axis_index("lat"), lax.axis_index("lon")
    assert batch == 1 and lons % 2 == 0
    coarse_rows, half = rows // 2, cols // 2
    cells = coarse_rows * half
    pairs = coarse_rows + 1
    fine = 4 * channels
    lanes = 2 * channels
    scale = 1.0 / math.sqrt(batch * rows * cols * lats * lons)
    first_half = lon < lons // 2
    flags = jnp.stack(
        [first_half, lon % 2 == 1, lat == 0, lat == lats - 1]
    ).astype(jnp.int32)

    cot = cotangent.reshape(channels, rows, cols)
    x = coarse_field.transpose(0, 2, 3, 1).reshape(cells, in_channels)
    up_w = tconv_weight.reshape(fine, in_channels)

    top, bottom = cot[:, 0], cot[:, rows - 1]
    there, back = row_routes(lats, lons)
    row_a = lax.ppermute(jnp.where(first_half, bottom, top), AXES, there)
    row_b = lax.ppermute(jnp.where(first_half, top, bottom), AXES, back)

    near, send_a, send_b = pl.pallas_call(
        gather_kernel,
        out_shape=(
            jax.ShapeDtypeStruct((pairs, 4 * half, lanes), BF16),
            jax.ShapeDtypeStruct((pairs, lanes), BF16),
            jax.ShapeDtypeStruct((pairs, lanes), BF16),
        ),
        in_specs=[SMEM, VMEM, VMEM, VMEM],
        out_specs=(VMEM, VMEM, VMEM),
        scratch_shapes=[
            pltpu.VMEM((channels * rows, cols), F32),
            pltpu.VMEM((2, pairs, lanes), F32),
        ],
        name="gather_rows",
    )(flags, cot, row_a, row_b)

    inner = [(i, i ^ 1) for i in range(lons)]
    outer = [(i, (i + (1 if i % 2 else -1)) % lons) for i in range(lons)]
    col_a = lax.ppermute(send_a, "lon", inner)
    col_b = lax.ppermute(send_b, "lon", outer)

    grad, sums = pl.pallas_call(
        main_kernel,
        out_shape=(
            jax.ShapeDtypeStruct((cells, in_channels), BF16),
            jax.ShapeDtypeStruct((fine + 5 * channels, lanes), F32),
        ),
        in_specs=[SMEM, VMEM, pl.BlockSpec(memory_space=pl.ANY), VMEM, VMEM, VMEM, VMEM],
        out_specs=(VMEM, VMEM),
        scratch_shapes=[
            pltpu.VMEM((pairs, 4 * half, lanes), BF16),
            pltpu.VMEM((2, 4 * half, lanes), BF16),
            pltpu.VMEM((2, pairs, lanes), F32),
            pltpu.VMEM((4, fine, fine), BF16),
            pltpu.VMEM((4, fine, fine), F32),
            pltpu.VMEM((fine, in_channels), F32),
            pltpu.VMEM((4 * half, fine), F32),
            pltpu.SemaphoreType.DMA,
        ],
        name="section",
    )(flags, x, near, col_a, col_b, up_w, conv_weight)

    whole = summed_everywhere(sums, scale)
    tconv_grad = whole[:fine].reshape(4, channels, in_channels)
    blocks = whole[fine:].reshape(5, channels, lanes)
    conv_grad = jnp.concatenate([blocks[u] for u in range(5)], axis=1)[:, : 9 * channels]
    coarse_grad = grad.reshape(1, coarse_rows, half, in_channels).transpose(0, 3, 1, 2)
    return (coarse_grad, tconv_grad, conv_grad)


def solution(mesh):
    return jax.shard_map(
        per_device,
        mesh=mesh,
        in_specs=(P(None, None, "lat", "lon"), P(None, None, "lat", "lon"), P(), P()),
        out_specs=(P(None, None, "lat", "lon"), P(), P()),
        check_vma=False,
    )
```

```python
import math

import jax
import jax.numpy as jnp
from jax import lax
from jax.experimental import pallas as pl
from jax.experimental.pallas import tpu as pltpu
from jax.sharding import PartitionSpec as P

F32, BF16 = jnp.float32, jnp.bfloat16
AXES = ("lat", "lon")
SHIFTS = (-1, 0, 1, 2)
VMEM = pl.BlockSpec(memory_space=pltpu.VMEM)
LIMIT = pltpu.CompilerParams(vmem_limit_bytes=24 * 2**20)


def product(lhs, rhs, lhs_dim, rhs_dim):
    dims = (((lhs_dim,), (rhs_dim,)), ((), ()))
    return lax.dot_general(lhs, rhs, dims, preferred_element_type=F32)


def resident(array):
    return pltpu.with_memory_space_constraint(array, pltpu.VMEM)


def place_weights(conv_w, weights, packed):
    channels, width = conv_w.shape
    pair = 2 * channels
    packed[0, :, 0:width] = conv_w[...]
    packed[1, :, 0 : width - channels] = conv_w[:, channels:width]
    weights[...] = jnp.zeros_like(weights)
    for e in range(4):
        for p in range(2):
            a = p - SHIFTS[e]
            if abs(a) > 1:
                continue
            tap = 3 * (a + 1)
            rows = slice(e * channels, (e + 1) * channels)
            low = p * pair
            for d in range(4):
                first = tap - SHIFTS[d] + 1
                if d == 0:
                    base = packed[first % 2, :, (first - first % 2) * channels :][:, 0:channels]
                    weights[d, rows, low : low + channels] = base
                elif d == 3:
                    weights[d, rows, low + channels : low + pair] = conv_w[
                        :, tap * channels : (tap + 1) * channels
                    ]
                else:
                    start = (first - first % 2) * channels
                    weights[d, rows, low : low + pair] = packed[
                        first % 2, :, start : start + pair
                    ]


def up_kernel(x, up_w, conv_w, slope, act_t, act_rim, weights, packed):
    fine = up_w.shape[0]
    rows = act_rim.shape[1]
    half = x.shape[0] // rows
    group = math.gcd(rows, 8)
    cells = group * half
    place_weights(conv_w, weights, packed)

    def step(s, carry):
        start = pl.multiple_of(s * cells, cells)
        up = product(x[pl.ds(start, cells), :], up_w[...], 1, 1)
        gate = 1.0 / (1.0 + jnp.exp(-up))
        active = up * gate
        slope[pl.ds(start, cells), :] = gate * (1.0 + up * (1.0 - gate))
        act_t[:, pl.ds(start, cells)] = active.astype(BF16).T
        for k in range(group):
            at = pl.ds(s * group + k, 1)
            act_rim[0, at, :] = active[k * half : k * half + 1]
            act_rim[1, at, :] = active[(k + 1) * half - 1 : (k + 1) * half]
        return carry

    lax.fori_loop(0, rows // group, step, 0)


def gather_kernel(cot, recv_a, recv_b, after, near, polar, send_a, send_b, edges):
    rows, channels, cols = cot.shape
    half = cols // 2
    pairs = near.shape[0]
    first_half = 2 * lax.axis_index("lon") < lax.axis_size("lon")
    odd = lax.rem(lax.axis_index("lon"), 2) == 1
    at_north = lax.axis_index("lat") == 0
    at_south = lax.axis_index("lat") == lax.axis_size("lat") - 1
    row_id = lax.broadcasted_iota(jnp.int32, (4 * half, cols), 0)
    col_id = lax.broadcasted_iota(jnp.int32, (4 * half, cols), 1)
    pick = jnp.where(col_id == 2 * (row_id % half) + row_id // half - 1, 1.0, 0.0)
    pick = pick.astype(BF16)
    from_a = recv_a[...].astype(F32)
    from_b = recv_b[...].astype(F32)
    top = jnp.where(first_half, from_a, from_b).astype(BF16)
    bottom = jnp.where(first_half, from_b, from_a).astype(BF16)

    def keep_edges(m, block):
        edges[0, pl.ds(m, 1), :] = block[half : half + 1]
        edges[1, pl.ds(m, 1), :] = block[3 * half - 1 : 3 * half]

    def middle(q, carry):
        m = 1 + 2 * q
        four = cot[pl.ds(2 * m - 1, 4)].reshape(4 * channels, cols)
        out = product(pick, four, 1, 1)
        for k in range(2):
            block = out[:, k * 2 * channels : (k + 1) * 2 * channels]
            near[m + k] = block.astype(BF16)
            keep_edges(m + k, block)
        return carry

    lane_id = lax.broadcasted_iota(jnp.int32, (4 * half, 2 * channels), 1)
    ends = ((0, top, cot[0], at_north), (pairs - 1, cot[rows - 1], bottom, at_south))
    for side, (m, one, two, pole) in enumerate(ends):
        block = product(pick, jnp.concatenate([one, two], axis=0), 1, 1)
        keep_edges(m, block)
        beyond = (lane_id < channels) if side == 0 else (lane_id >= channels)
        away = jnp.where(jnp.logical_and(beyond, pole), block, 0.0)
        polar[side] = away.astype(BF16)
        near[m] = (block - away).astype(BF16)
    lax.fori_loop(0, (pairs - 3) // 2, middle, 0, unroll=3)
    m = pairs - 2
    block = product(pick, cot[2 * m - 1 : 2 * m + 1].reshape(2 * channels, cols), 1, 1)
    near[m] = block.astype(BF16)
    keep_edges(m, block)
    send_a[...] = jnp.where(odd, edges[0], edges[1]).astype(BF16)
    send_b[...] = jnp.where(odd, edges[1], edges[0]).astype(BF16)


def spread_kernel(near, polar, act_t, weights, feature, conv_acc):
    pairs, quad, lanes = near.shape
    half, rows, fine = quad // 4, pairs - 1, weights.shape[1]
    group = math.gcd(rows, 8)
    cells = group * half
    all_w = weights[...].reshape(4 * fine, fine)

    def around(first, count, d):
        piece = slice(d * half, (d + 1) * half)
        lower = near[pl.ds(first, count), piece, :].reshape(count * half, lanes)
        upper = near[pl.ds(first + 1, count), piece, :].reshape(count * half, lanes)
        return [lower, upper]

    def step(s, carry):
        parts = []
        for d in range(4):
            parts += around(s * group, group, d)
        start = pl.multiple_of(s * cells, cells)
        feature[pl.ds(start, cells), :] = product(jnp.concatenate(parts, axis=1), all_w, 1, 0)
        return carry

    lax.fori_loop(0, rows // group, step, 0)
    for d in range(4):
        conv_acc[d] = product(act_t[...], jnp.concatenate(around(0, rows, d), axis=1), 1, 0)

    @pl.when(lax.axis_index("lat") == 0)
    def _():
        for d in range(4):
            cap = polar[0, d * half : (d + 1) * half, :]
            feature[0:half, 0:lanes] += product(cap, weights[d, lanes:fine, 0:lanes], 1, 0)
            conv_acc[d, 0:lanes, lanes:fine] += product(act_t[0:lanes, 0:half], cap, 1, 0)

    @pl.when(lax.axis_index("lat") == lax.axis_size("lat") - 1)
    def _():
        last = rows * half
        for d in range(4):
            cap = polar[1, d * half : (d + 1) * half, :]
            feature[last - half : last, lanes:fine] += product(
                cap, weights[d, 0:lanes, lanes:fine], 1, 0
            )
            padded = jnp.concatenate([jnp.zeros_like(cap), cap], axis=0)
            conv_acc[d, lanes:fine, 0:lanes] += product(
                act_t[lanes:fine, last - 2 * half : last], padded, 1, 0
            )


def finish_kernel(x, feature, slope, conv_acc, act_rim, col_a, col_b, weights, up_w,
                  grad, sums, extra, rims, rim_feature, rim_conv, up_acc):
    rows = act_rim.shape[1]
    fine, lanes = weights.shape[1], rims.shape[2]
    channels = lanes // 2
    half = x.shape[0] // rows
    group = math.gcd(rows, 8)
    cells = group * half
    odd = lax.rem(lax.axis_index("lon"), 2) == 1
    at_north = lax.axis_index("lat") == 0
    at_south = lax.axis_index("lat") == lax.axis_size("lat") - 1
    from_a = col_a[...].astype(F32)
    from_b = col_b[...].astype(F32)
    rims[0] = jnp.where(odd, from_a, from_b)
    rims[1] = jnp.where(odd, from_b, from_a)
    extra[...] = jnp.zeros_like(extra)
    up_acc[...] = jnp.zeros_like(up_acc)
    row_id = lax.broadcasted_iota(jnp.int32, (rows, lanes), 0)
    lane_id = lax.broadcasted_iota(jnp.int32, (rows, lanes), 1)
    top_corner = jnp.logical_and(row_id == 0, lane_id < channels)
    end_corner = jnp.logical_and(row_id == rows - 1, lane_id >= channels)
    for side, d in ((0, 0), (1, 3)):
        lower, upper = rims[side, 0:rows, :], rims[side, 1 : rows + 1, :]
        lower = jnp.where(jnp.logical_and(top_corner, at_north), 0.0, lower)
        upper = jnp.where(jnp.logical_and(end_corner, at_south), 0.0, upper)
        ring = jnp.concatenate([lower, upper], axis=1).astype(BF16)
        rim_feature[side] = product(ring, weights[d], 1, 0)
        rim_conv[side] = product(act_rim[side].astype(BF16), ring, 0, 0)

    def corner(mask, offset, low, high, swap):
        for side, d in ((0, 0), (1, 3)):
            piece = jnp.where(mask, rims[side, offset : offset + rows, :], 0.0)
            blank = jnp.zeros_like(piece)
            parts = [blank, piece] if swap else [piece, blank]
            cap = jnp.concatenate(parts, axis=1).astype(BF16)
            rim_feature[side, :, low:high] += product(cap, weights[d, :, low:high], 1, 0)
            rim_conv[side, low:high, :] += product(
                act_rim[side, :, low:high].astype(BF16), cap, 0, 0
            )

    @pl.when(at_north)
    def _():
        corner(top_corner, 0, 0, lanes, True)

    @pl.when(at_south)
    def _():
        corner(end_corner, 1, lanes, fine, False)

    def step(s, carry):
        start = pl.multiple_of(s * cells, cells)
        for k in range(group):
            at = pl.ds(s * group + k, 1)
            extra[k * half : k * half + 1, :] = rim_feature[0, at, :]
            extra[(k + 1) * half - 1 : (k + 1) * half, :] = rim_feature[1, at, :]
        whole = feature[pl.ds(start, cells), :] + extra[...]
        pre = (whole * slope[pl.ds(start, cells), :]).astype(BF16)
        grad[pl.ds(start, cells), :] = product(pre, up_w[...], 1, 0).astype(BF16)
        up_acc[...] += product(pre, x[pl.ds(start, cells), :], 0, 0)
        return carry

    lax.fori_loop(0, rows // group, step, 0)
    sums[0:fine, :] = up_acc[...]

    def part(d, block):
        at = slice(block * channels, (block + 1) * channels)
        value = conv_acc[d, at, :]
        if d == 0:
            value = value + rim_conv[0, at, :]
        if d == 3:
            value = value + rim_conv[1, at, :]
        return value

    taps = []
    for b in (-1, 0, 1):
        upper = part(1 - b, 0) + part(2 - b, 1)
        lower = part(1 - b, 2) + part(2 - b, 3)
        taps.append(upper + pltpu.roll(lower, fine - channels, 1))
    turned = jnp.concatenate(taps[0:2], axis=0).T
    sums[fine : fine + 3 * channels, :] = turned[0 : 3 * channels]
    turned = jnp.concatenate([taps[2], pltpu.roll(taps[2], fine - channels, 1)], axis=0).T
    sums[fine + 3 * channels : fine + 4 * channels, :] = turned[0:channels]
    sums[fine + 4 * channels : fine + 5 * channels, :] = turned[2 * channels : 3 * channels]


def summed_everywhere(part, scale):
    members = lax.axis_size(AXES)
    rows, lanes = part.shape
    piece = -(-rows // members)
    if members * piece > rows:
        part = jnp.pad(part, ((0, members * piece - rows), (0, 0)))
    parts = lax.all_to_all(part.reshape(members, piece * lanes), AXES, 0, 0, tiled=True)
    own = jnp.sum(parts, axis=0) * scale
    spread = jnp.broadcast_to(own[None], (members, piece * lanes))
    whole = lax.all_to_all(spread, AXES, 0, 0, tiled=True)
    return whole.reshape(members * piece, lanes)[:rows]


def row_routes(lats, lons):
    half = lons // 2
    there = []
    for lat in range(lats):
        for lon in range(lons):
            if lon < half:
                target = (lat + 1, lon) if lat + 1 < lats else (lat, lon + half)
            else:
                target = (lat - 1, lon) if lat > 0 else (lat, lon - half)
            there.append((lat * lons + lon, target[0] * lons + target[1]))
    return there, [(b, a) for a, b in there]


def per_device(coarse_field, cotangent, tconv_weight, conv_weight):
    batch, channels, rows, cols = cotangent.shape
    in_channels = coarse_field.shape[1]
    lats, lons = lax.axis_size("lat"), lax.axis_size("lon")
    assert batch == 1 and lons % 2 == 0
    coarse_rows, half = rows // 2, cols // 2
    cells = coarse_rows * half
    pairs = coarse_rows + 1
    fine = 4 * channels
    lanes = 2 * channels
    scale = 1.0 / math.sqrt(batch * rows * cols * lats * lons)
    group = math.gcd(coarse_rows, 8)

    cot = cotangent.reshape(channels, rows, cols).transpose(1, 0, 2)
    x = coarse_field.transpose(0, 2, 3, 1).reshape(cells, in_channels)
    up_w = tconv_weight.reshape(fine, in_channels)

    first_half = lax.axis_index("lon") < lons // 2
    top, bottom = cot[0], cot[rows - 1]
    there, back = row_routes(lats, lons)
    row_a = lax.ppermute(jnp.where(first_half, bottom, top), AXES, there)
    row_b = lax.ppermute(jnp.where(first_half, top, bottom), AXES, back)

    slope, act_t, act_rim, weights = pl.pallas_call(
        up_kernel,
        out_shape=(
            pltpu.VMEM((cells, fine), F32),
            pltpu.VMEM((fine, cells), BF16),
            pltpu.VMEM((2, coarse_rows, fine), F32),
            pltpu.VMEM((4, fine, fine), BF16),
        ),
        in_specs=[VMEM] * 3,
        out_specs=(VMEM,) * 4,
        scratch_shapes=[pltpu.VMEM((2, channels, 10 * channels), BF16)],
        compiler_params=LIMIT,
        name="up",
    )(x, up_w, conv_weight)
    slope, act_t, act_rim, weights = map(resident, (slope, act_t, act_rim, weights))

    near, polar, send_a, send_b = pl.pallas_call(
        gather_kernel,
        out_shape=(
            pltpu.VMEM((pairs, 4 * half, lanes), BF16),
            pltpu.VMEM((2, 4 * half, lanes), BF16),
            pltpu.VMEM((pairs, lanes), BF16),
            pltpu.VMEM((pairs, lanes), BF16),
        ),
        in_specs=[VMEM] * 4,
        out_specs=(VMEM,) * 4,
        scratch_shapes=[pltpu.VMEM((2, pairs, lanes), F32)],
        compiler_params=LIMIT,
        name="gather",
    )(resident(cot), resident(row_a), resident(row_b), act_rim)

    inner = [(i, i ^ 1) for i in range(lons)]
    outer = [(i, (i + (1 if i % 2 else -1)) % lons) for i in range(lons)]
    col_a = lax.ppermute(send_a, "lon", inner)
    col_b = lax.ppermute(send_b, "lon", outer)

    feature, conv_acc = pl.pallas_call(
        spread_kernel,
        out_shape=(pltpu.VMEM((cells, fine), F32), pltpu.VMEM((4, fine, fine), F32)),
        in_specs=[VMEM] * 4,
        out_specs=(VMEM,) * 2,
        compiler_params=LIMIT,
        name="spread",
    )(resident(near), resident(polar), act_t, weights)

    grad, sums = pl.pallas_call(
        finish_kernel,
        out_shape=(
            jax.ShapeDtypeStruct((cells, in_channels), BF16),
            pltpu.VMEM((fine + 5 * channels, lanes), F32),
        ),
        in_specs=[VMEM] * 9,
        out_specs=(VMEM,) * 2,
        scratch_shapes=[
            pltpu.VMEM((group * half, fine), F32),
            pltpu.VMEM((2, pairs, lanes), F32),
            pltpu.VMEM((2, coarse_rows, fine), F32),
            pltpu.VMEM((2, fine, fine), F32),
            pltpu.VMEM((fine, in_channels), F32),
        ],
        compiler_params=LIMIT,
        name="finish",
    )(
        x, resident(feature), slope, resident(conv_acc), act_rim,
        resident(col_a), resident(col_b), weights, up_w,
    )

    whole = summed_everywhere(sums, scale)
    tconv_grad = whole[:fine].reshape(4, channels, in_channels)
    blocks = whole[fine:].reshape(5, channels, lanes)
    both, last = blocks[3], blocks[4]
    conv_grad = jnp.concatenate(
        [
            blocks[2], last[:, :channels],
            blocks[1], both[:, channels:],
            blocks[0], both[:, :channels],
        ],
        axis=1,
    )
    coarse_grad = grad.reshape(1, coarse_rows, half, in_channels).transpose(0, 3, 1, 2)
    return (coarse_grad, tconv_grad, conv_grad)


def solution(mesh):
    return jax.shard_map(
        per_device,
        mesh=mesh,
        in_specs=(P(None, None, "lat", "lon"), P(None, None, "lat", "lon"), P(), P()),
        out_specs=(P(None, None, "lat", "lon"), P(), P()),
        check_vma=False,
    )
```

```python
import math

import jax
import jax.numpy as jnp
from jax import lax
from jax.experimental import pallas as pl
from jax.experimental.pallas import tpu as pltpu
from jax.sharding import PartitionSpec as P

F32, BF16 = jnp.float32, jnp.bfloat16
AXES = ("lat", "lon")
SHIFTS = (-1, 0, 1, 2)
VMEM = pl.BlockSpec(memory_space=pltpu.VMEM)
LIMIT = pltpu.CompilerParams(vmem_limit_bytes=24 * 2**20)


def product(lhs, rhs, lhs_dim, rhs_dim):
    dims = (((lhs_dim,), (rhs_dim,)), ((), ()))
    return lax.dot_general(lhs, rhs, dims, preferred_element_type=F32)


def resident(array):
    return pltpu.with_memory_space_constraint(array, pltpu.VMEM)


def place_weights(conv_w, weights, packed):
    channels, width = conv_w.shape
    pair = 2 * channels
    packed[0, :, 0:width] = conv_w[...]
    packed[1, :, 0 : width - channels] = conv_w[:, channels:width]
    weights[...] = jnp.zeros_like(weights)
    for e in range(4):
        for p in range(2):
            a = p - SHIFTS[e]
            if abs(a) > 1:
                continue
            tap = 3 * (a + 1)
            rows = slice(e * channels, (e + 1) * channels)
            low = p * pair
            for d in range(4):
                first = tap - SHIFTS[d] + 1
                if d == 0:
                    base = packed[first % 2, :, (first - first % 2) * channels :][:, 0:channels]
                    weights[d, rows, low : low + channels] = base
                elif d == 3:
                    weights[d, rows, low + channels : low + pair] = conv_w[
                        :, tap * channels : (tap + 1) * channels
                    ]
                else:
                    start = (first - first % 2) * channels
                    weights[d, rows, low : low + pair] = packed[
                        first % 2, :, start : start + pair
                    ]


def up_kernel(x, up_w, conv_w, slope, act_t, act_rim, weights, packed):
    fine = up_w.shape[0]
    rows = act_rim.shape[1]
    half = x.shape[0] // rows
    group = math.gcd(rows, 8)
    cells = group * half
    place_weights(conv_w, weights, packed)

    def step(s, carry):
        start = pl.multiple_of(s * cells, cells)
        up = product(x[pl.ds(start, cells), :], up_w[...], 1, 1)
        gate = 1.0 / (1.0 + jnp.exp(-up))
        active = up * gate
        slope[pl.ds(start, cells), :] = gate * (1.0 + up * (1.0 - gate))
        act_t[:, pl.ds(start, cells)] = active.astype(BF16).T
        for k in range(group):
            at = pl.ds(s * group + k, 1)
            act_rim[0, at, :] = active[k * half : k * half + 1]
            act_rim[1, at, :] = active[(k + 1) * half - 1 : (k + 1) * half]
        return carry

    lax.fori_loop(0, rows // group, step, 0)


def gather_kernel(cot, recv_a, recv_b, after, near, polar, send_a, send_b, edges):
    rows, channels, cols = cot.shape
    half = cols // 2
    pairs = near.shape[0]
    first_half = 2 * lax.axis_index("lon") < lax.axis_size("lon")
    odd = lax.rem(lax.axis_index("lon"), 2) == 1
    at_north = lax.axis_index("lat") == 0
    at_south = lax.axis_index("lat") == lax.axis_size("lat") - 1
    row_id = lax.broadcasted_iota(jnp.int32, (4 * half, cols), 0)
    col_id = lax.broadcasted_iota(jnp.int32, (4 * half, cols), 1)
    pick = jnp.where(col_id == 2 * (row_id % half) + row_id // half - 1, 1.0, 0.0)
    pick = pick.astype(BF16)
    from_a = recv_a[...].astype(F32)
    from_b = recv_b[...].astype(F32)
    top = jnp.where(first_half, from_a, from_b).astype(BF16)
    bottom = jnp.where(first_half, from_b, from_a).astype(BF16)

    def keep_edges(m, block):
        edges[0, pl.ds(m, 1), :] = block[half : half + 1]
        edges[1, pl.ds(m, 1), :] = block[3 * half - 1 : 3 * half]

    def middle(q, carry):
        m = 1 + 2 * q
        four = cot[pl.ds(2 * m - 1, 4)].reshape(4 * channels, cols)
        out = product(pick, four, 1, 1)
        for k in range(2):
            block = out[:, k * 2 * channels : (k + 1) * 2 * channels]
            near[m + k] = block.astype(BF16)
            keep_edges(m + k, block)
        return carry

    lane_id = lax.broadcasted_iota(jnp.int32, (4 * half, 2 * channels), 1)
    ends = ((0, top, cot[0], at_north), (pairs - 1, cot[rows - 1], bottom, at_south))
    for side, (m, one, two, pole) in enumerate(ends):
        block = product(pick, jnp.concatenate([one, two], axis=0), 1, 1)
        keep_edges(m, block)
        beyond = (lane_id < channels) if side == 0 else (lane_id >= channels)
        away = jnp.where(jnp.logical_and(beyond, pole), block, 0.0)
        polar[side] = away.astype(BF16)
        near[m] = (block - away).astype(BF16)
    lax.fori_loop(0, (pairs - 3) // 2, middle, 0, unroll=3)
    m = pairs - 2
    block = product(pick, cot[2 * m - 1 : 2 * m + 1].reshape(2 * channels, cols), 1, 1)
    near[m] = block.astype(BF16)
    keep_edges(m, block)
    send_a[...] = jnp.where(odd, edges[0], edges[1]).astype(BF16)
    send_b[...] = jnp.where(odd, edges[1], edges[0]).astype(BF16)


def spread_kernel(near, polar, act_t, weights, feature, conv_acc):
    pairs, quad, lanes = near.shape
    half, rows, fine = quad // 4, pairs - 1, weights.shape[1]
    group = math.gcd(rows, 8)
    cells = group * half
    all_w = weights[...].reshape(4 * fine, fine)

    def around(first, count, d):
        piece = slice(d * half, (d + 1) * half)
        lower = near[pl.ds(first, count), piece, :].reshape(count * half, lanes)
        upper = near[pl.ds(first + 1, count), piece, :].reshape(count * half, lanes)
        return [lower, upper]

    def step(s, carry):
        parts = []
        for d in range(4):
            parts += around(s * group, group, d)
        start = pl.multiple_of(s * cells, cells)
        feature[pl.ds(start, cells), :] = product(jnp.concatenate(parts, axis=1), all_w, 1, 0)
        return carry

    lax.fori_loop(0, rows // group, step, 0)
    for d in range(4):
        conv_acc[d] = product(act_t[...], jnp.concatenate(around(0, rows, d), axis=1), 1, 0)

    @pl.when(lax.axis_index("lat") == 0)
    def _():
        for d in range(4):
            cap = polar[0, d * half : (d + 1) * half, :]
            feature[0:half, 0:lanes] += product(cap, weights[d, lanes:fine, 0:lanes], 1, 0)
            conv_acc[d, 0:lanes, lanes:fine] += product(act_t[0:lanes, 0:half], cap, 1, 0)

    @pl.when(lax.axis_index("lat") == lax.axis_size("lat") - 1)
    def _():
        last = rows * half
        for d in range(4):
            cap = polar[1, d * half : (d + 1) * half, :]
            feature[last - half : last, lanes:fine] += product(
                cap, weights[d, 0:lanes, lanes:fine], 1, 0
            )
            padded = jnp.concatenate([jnp.zeros_like(cap), cap], axis=0)
            conv_acc[d, lanes:fine, 0:lanes] += product(
                act_t[lanes:fine, last - 2 * half : last], padded, 1, 0
            )


def finish_kernel(x, feature, slope, conv_acc, act_rim, col_a, col_b, weights, up_w,
                  grad, sums, extra, rims, rim_feature, rim_conv, up_acc):
    rows = act_rim.shape[1]
    fine, lanes = weights.shape[1], rims.shape[2]
    channels = lanes // 2
    half = x.shape[0] // rows
    group = math.gcd(rows, 8)
    cells = group * half
    odd = lax.rem(lax.axis_index("lon"), 2) == 1
    at_north = lax.axis_index("lat") == 0
    at_south = lax.axis_index("lat") == lax.axis_size("lat") - 1
    from_a = col_a[...].astype(F32)
    from_b = col_b[...].astype(F32)
    rims[0] = jnp.where(odd, from_a, from_b)
    rims[1] = jnp.where(odd, from_b, from_a)
    extra[...] = jnp.zeros_like(extra)
    up_acc[...] = jnp.zeros_like(up_acc)
    row_id = lax.broadcasted_iota(jnp.int32, (rows, lanes), 0)
    lane_id = lax.broadcasted_iota(jnp.int32, (rows, lanes), 1)
    top_corner = jnp.logical_and(row_id == 0, lane_id < channels)
    end_corner = jnp.logical_and(row_id == rows - 1, lane_id >= channels)
    for side, d in ((0, 0), (1, 3)):
        lower, upper = rims[side, 0:rows, :], rims[side, 1 : rows + 1, :]
        lower = jnp.where(jnp.logical_and(top_corner, at_north), 0.0, lower)
        upper = jnp.where(jnp.logical_and(end_corner, at_south), 0.0, upper)
        ring = jnp.concatenate([lower, upper], axis=1).astype(BF16)
        rim_feature[side] = product(ring, weights[d], 1, 0)
        rim_conv[side] = product(act_rim[side].astype(BF16), ring, 0, 0)

    def corner(mask, offset, low, high, swap):
        for side, d in ((0, 0), (1, 3)):
            piece = jnp.where(mask, rims[side, offset : offset + rows, :], 0.0)
            blank = jnp.zeros_like(piece)
            parts = [blank, piece] if swap else [piece, blank]
            cap = jnp.concatenate(parts, axis=1).astype(BF16)
            rim_feature[side, :, low:high] += product(cap, weights[d, :, low:high], 1, 0)
            rim_conv[side, low:high, :] += product(
                act_rim[side, :, low:high].astype(BF16), cap, 0, 0
            )

    @pl.when(at_north)
    def _():
        corner(top_corner, 0, 0, lanes, True)

    @pl.when(at_south)
    def _():
        corner(end_corner, 1, lanes, fine, False)

    def step(s, carry):
        start = pl.multiple_of(s * cells, cells)
        for k in range(group):
            at = pl.ds(s * group + k, 1)
            extra[k * half : k * half + 1, :] = rim_feature[0, at, :]
            extra[(k + 1) * half - 1 : (k + 1) * half, :] = rim_feature[1, at, :]
        whole = feature[pl.ds(start, cells), :] + extra[...]
        pre = (whole * slope[pl.ds(start, cells), :]).astype(BF16)
        grad[pl.ds(start, cells), :] = product(pre, up_w[...], 1, 0).astype(BF16)
        up_acc[...] += product(pre, x[pl.ds(start, cells), :], 0, 0)
        return carry

    lax.fori_loop(0, rows // group, step, 0)
    sums[0:fine, :] = up_acc[...].astype(BF16)

    def part(d, block):
        at = slice(block * channels, (block + 1) * channels)
        value = conv_acc[d, at, :]
        if d == 0:
            value = value + rim_conv[0, at, :]
        if d == 3:
            value = value + rim_conv[1, at, :]
        return value

    taps = []
    for b in (-1, 0, 1):
        upper = part(1 - b, 0) + part(2 - b, 1)
        lower = part(1 - b, 2) + part(2 - b, 3)
        taps.append(upper + pltpu.roll(lower, fine - channels, 1))
    turned = jnp.concatenate(taps[0:2], axis=0).T
    sums[fine : fine + 3 * channels, :] = turned[0 : 3 * channels].astype(BF16)
    turned = jnp.concatenate([taps[2], pltpu.roll(taps[2], fine - channels, 1)], axis=0).T
    sums[fine + 3 * channels : fine + 4 * channels, :] = turned[0:channels].astype(BF16)
    sums[fine + 4 * channels : fine + 5 * channels, :] = turned[2 * channels : 3 * channels].astype(BF16)


def unpack_kernel(whole, tconv_grad, conv_grad):
    fine, lanes = tconv_grad.shape
    channels = conv_grad.shape[0]
    tconv_grad[...] = whole[0:fine].astype(F32)
    block = [
        whole[fine + k * channels : fine + (k + 1) * channels].astype(F32) for k in range(5)
    ]
    singles = (block[4][:, :channels], block[3][:, channels:], block[3][:, :channels])
    for a in range(3):
        start = 3 * a * channels
        conv_grad[:, start : start + lanes] = block[2 - a]
        conv_grad[:, start + lanes : start + lanes + channels] = singles[a]


def summed_everywhere(part, scale):
    members = lax.axis_size(AXES)
    rows, lanes = part.shape
    piece = -(-rows // members)
    if members * piece > rows:
        part = jnp.pad(part, ((0, members * piece - rows), (0, 0)))
    parts = lax.all_to_all(part.reshape(members, piece, lanes), AXES, 0, 0, tiled=True)
    own = (jnp.sum(parts.astype(F32), axis=0) * scale).astype(part.dtype)
    spread = jnp.broadcast_to(own[None], (members, piece, lanes))
    whole = lax.all_to_all(spread, AXES, 0, 0, tiled=True)
    return whole.reshape(members * piece, lanes)[:rows]


def row_routes(lats, lons):
    half = lons // 2
    there = []
    for lat in range(lats):
        for lon in range(lons):
            if lon < half:
                target = (lat + 1, lon) if lat + 1 < lats else (lat, lon + half)
            else:
                target = (lat - 1, lon) if lat > 0 else (lat, lon - half)
            there.append((lat * lons + lon, target[0] * lons + target[1]))
    return there, [(b, a) for a, b in there]


def per_device(coarse_field, cotangent, tconv_weight, conv_weight):
    batch, channels, rows, cols = cotangent.shape
    in_channels = coarse_field.shape[1]
    lats, lons = lax.axis_size("lat"), lax.axis_size("lon")
    assert batch == 1 and lons % 2 == 0
    coarse_rows, half = rows // 2, cols // 2
    cells = coarse_rows * half
    pairs = coarse_rows + 1
    fine = 4 * channels
    lanes = 2 * channels
    scale = 1.0 / math.sqrt(batch * rows * cols * lats * lons)
    group = math.gcd(coarse_rows, 8)

    cot = cotangent.reshape(channels, rows, cols).transpose(1, 0, 2)
    x = coarse_field.transpose(0, 2, 3, 1).reshape(cells, in_channels)
    up_w = tconv_weight.reshape(fine, in_channels)

    first_half = lax.axis_index("lon") < lons // 2
    top, bottom = cot[0], cot[rows - 1]
    there, back = row_routes(lats, lons)
    row_a = lax.ppermute(jnp.where(first_half, bottom, top), AXES, there)
    row_b = lax.ppermute(jnp.where(first_half, top, bottom), AXES, back)

    slope, act_t, act_rim, weights = pl.pallas_call(
        up_kernel,
        out_shape=(
            pltpu.VMEM((cells, fine), F32),
            pltpu.VMEM((fine, cells), BF16),
            pltpu.VMEM((2, coarse_rows, fine), F32),
            pltpu.VMEM((4, fine, fine), BF16),
        ),
        in_specs=[VMEM] * 3,
        out_specs=(VMEM,) * 4,
        scratch_shapes=[pltpu.VMEM((2, channels, 10 * channels), BF16)],
        compiler_params=LIMIT,
        name="up",
    )(x, up_w, conv_weight)
    slope, act_t, act_rim, weights = map(resident, (slope, act_t, act_rim, weights))

    near, polar, send_a, send_b = pl.pallas_call(
        gather_kernel,
        out_shape=(
            pltpu.VMEM((pairs, 4 * half, lanes), BF16),
            pltpu.VMEM((2, 4 * half, lanes), BF16),
            pltpu.VMEM((pairs, lanes), BF16),
            pltpu.VMEM((pairs, lanes), BF16),
        ),
        in_specs=[VMEM] * 4,
        out_specs=(VMEM,) * 4,
        scratch_shapes=[pltpu.VMEM((2, pairs, lanes), F32)],
        compiler_params=LIMIT,
        name="gather",
    )(resident(cot), resident(row_a), resident(row_b), act_rim)

    inner = [(i, i ^ 1) for i in range(lons)]
    outer = [(i, (i + (1 if i % 2 else -1)) % lons) for i in range(lons)]
    col_a = lax.ppermute(send_a, "lon", inner)
    col_b = lax.ppermute(send_b, "lon", outer)

    feature, conv_acc = pl.pallas_call(
        spread_kernel,
        out_shape=(pltpu.VMEM((cells, fine), F32), pltpu.VMEM((4, fine, fine), F32)),
        in_specs=[VMEM] * 4,
        out_specs=(VMEM,) * 2,
        compiler_params=LIMIT,
        name="spread",
    )(resident(near), resident(polar), act_t, weights)

    grad, sums = pl.pallas_call(
        finish_kernel,
        out_shape=(
            jax.ShapeDtypeStruct((cells, in_channels), BF16),
            pltpu.VMEM((fine + 5 * channels, lanes), BF16),
        ),
        in_specs=[VMEM] * 9,
        out_specs=(VMEM,) * 2,
        scratch_shapes=[
            pltpu.VMEM((group * half, fine), F32),
            pltpu.VMEM((2, pairs, lanes), F32),
            pltpu.VMEM((2, coarse_rows, fine), F32),
            pltpu.VMEM((2, fine, fine), F32),
            pltpu.VMEM((fine, in_channels), F32),
        ],
        compiler_params=LIMIT,
        name="finish",
    )(
        x, resident(feature), slope, resident(conv_acc), act_rim,
        resident(col_a), resident(col_b), weights, up_w,
    )

    whole = summed_everywhere(sums, scale)
    tconv_grad, conv_grad = pl.pallas_call(
        unpack_kernel,
        out_shape=(
            jax.ShapeDtypeStruct((fine, in_channels), F32),
            jax.ShapeDtypeStruct((channels, 9 * channels), F32),
        ),
        in_specs=[VMEM],
        out_specs=(VMEM,) * 2,
        compiler_params=LIMIT,
        name="unpack",
    )(resident(whole))
    tconv_grad = tconv_grad.reshape(4, channels, in_channels)
    coarse_grad = grad.reshape(1, coarse_rows, half, in_channels).transpose(0, 3, 1, 2)
    return (coarse_grad, tconv_grad, conv_grad)


def solution(mesh):
    return jax.shard_map(
        per_device,
        mesh=mesh,
        in_specs=(P(None, None, "lat", "lon"), P(None, None, "lat", "lon"), P(), P()),
        out_specs=(P(None, None, "lat", "lon"), P(), P()),
        check_vma=False,
    )
```

```python
import math

import jax
import jax.numpy as jnp
from jax import lax
from jax.experimental import pallas as pl
from jax.experimental.pallas import tpu as pltpu
from jax.sharding import PartitionSpec as P

F32, BF16 = jnp.float32, jnp.bfloat16
AXES = ("lat", "lon")
SHIFTS = (-1, 0, 1, 2)
VMEM = pl.BlockSpec(memory_space=pltpu.VMEM)
LIMIT = pltpu.CompilerParams(vmem_limit_bytes=24 * 2**20)


def product(lhs, rhs, lhs_dim, rhs_dim):
    dims = (((lhs_dim,), (rhs_dim,)), ((), ()))
    return lax.dot_general(lhs, rhs, dims, preferred_element_type=F32)


def resident(array):
    return pltpu.with_memory_space_constraint(array, pltpu.VMEM)


def place_weights(conv_w, weights, packed):
    channels, width = conv_w.shape
    pair = 2 * channels
    packed[0, :, 0:width] = conv_w[...]
    packed[1, :, 0 : width - channels] = conv_w[:, channels:width]
    weights[...] = jnp.zeros_like(weights)
    for e in range(4):
        for p in range(2):
            a = p - SHIFTS[e]
            if abs(a) > 1:
                continue
            tap = 3 * (a + 1)
            rows = slice(e * channels, (e + 1) * channels)
            low = p * pair
            for d in range(4):
                first = tap - SHIFTS[d] + 1
                if d == 0:
                    base = packed[first % 2, :, (first - first % 2) * channels :][:, 0:channels]
                    weights[d, rows, low : low + channels] = base
                elif d == 3:
                    weights[d, rows, low + channels : low + pair] = conv_w[
                        :, tap * channels : (tap + 1) * channels
                    ]
                else:
                    start = (first - first % 2) * channels
                    weights[d, rows, low : low + pair] = packed[
                        first % 2, :, start : start + pair
                    ]


def up_kernel(x, up_w, conv_w, slope, act_t, act_rim, weights, packed):
    fine = up_w.shape[0]
    rows = act_rim.shape[1]
    half = x.shape[0] // rows
    group = math.gcd(rows, 8)
    cells = group * half
    place_weights(conv_w, weights, packed)

    def step(s, carry):
        start = pl.multiple_of(s * cells, cells)
        up = product(x[pl.ds(start, cells), :], up_w[...], 1, 1)
        gate = 1.0 / (1.0 + jnp.exp(-up))
        active = up * gate
        slope[pl.ds(start, cells), :] = gate * (1.0 + up * (1.0 - gate))
        act_t[:, pl.ds(start, cells)] = active.astype(BF16).T
        for k in range(group):
            at = pl.ds(s * group + k, 1)
            act_rim[0, at, :] = active[k * half : k * half + 1]
            act_rim[1, at, :] = active[(k + 1) * half - 1 : (k + 1) * half]
        return carry

    lax.fori_loop(0, rows // group, step, 0)


def gather_kernel(cot, after, near, pick, edges):
    rows, channels, cols = cot.shape
    half = cols // 2
    pairs = near.shape[0]
    row_id = lax.broadcasted_iota(jnp.int32, (4 * half, cols), 0)
    col_id = lax.broadcasted_iota(jnp.int32, (4 * half, cols), 1)
    hit = col_id == 2 * (row_id % half) + row_id // half - 1
    pick[...] = jnp.where(hit, 1.0, 0.0).astype(BF16)

    def emit(m, block):
        near[m] = block.astype(BF16)
        edges[0, pl.ds(m, 1), :] = block[half : half + 1]
        edges[1, pl.ds(m, 1), :] = block[3 * half - 1 : 3 * half]

    def middle(q, carry):
        m = 1 + 2 * q
        four = cot[pl.ds(2 * m - 1, 4)].reshape(4 * channels, cols)
        out = product(pick[...], four, 1, 1)
        emit(m, out[:, : 2 * channels])
        emit(m + 1, out[:, 2 * channels :])
        return carry

    lax.fori_loop(0, (pairs - 3) // 2, middle, 0, unroll=3)
    blank = jnp.zeros((channels, cols), BF16)
    two = [blank, cot[0], cot[rows - 1], blank]
    out = product(pick[...], jnp.concatenate(two, axis=0), 1, 1)
    emit(0, out[:, : 2 * channels])
    emit(pairs - 1, out[:, 2 * channels :])
    m = pairs - 2
    emit(m, product(pick[...], cot[2 * m - 1 : 2 * m + 1].reshape(2 * channels, cols), 1, 1))


def edge_kernel(recv_a, recv_b, pick, edges, caps, send_a, send_b):
    quad = caps.shape[1]
    half, pairs = quad // 4, edges.shape[1]
    channels = recv_a.shape[0]
    first_half = 2 * lax.axis_index("lon") < lax.axis_size("lon")
    odd = lax.rem(lax.axis_index("lon"), 2) == 1
    from_a = recv_a[...].astype(F32)
    from_b = recv_b[...].astype(F32)
    blank = jnp.zeros((channels, recv_a.shape[1]), BF16)
    top = jnp.where(first_half, from_a, from_b).astype(BF16)
    bottom = jnp.where(first_half, from_b, from_a).astype(BF16)
    out = product(pick[...], jnp.concatenate([top, blank, blank, bottom], axis=0), 1, 1)
    lanes = 2 * channels
    for side in range(2):
        caps[side] = out[:, side * lanes : (side + 1) * lanes].astype(BF16)
    row_id = lax.broadcasted_iota(jnp.int32, (pairs, lanes), 0)
    rim = []
    for side, at in ((0, half), (1, 3 * half - 1)):
        line = out[at : at + 1]
        rim.append(
            edges[side]
            + jnp.where(row_id == 0, line[:, :lanes], 0.0)
            + jnp.where(row_id == pairs - 1, line[:, lanes:], 0.0)
        )
    send_a[...] = jnp.where(odd, rim[0], rim[1]).astype(BF16)
    send_b[...] = jnp.where(odd, rim[1], rim[0]).astype(BF16)


def spread_kernel(near, caps, act_t, weights, feature, conv_acc):
    pairs, quad, lanes = near.shape
    half, rows, fine = quad // 4, pairs - 1, weights.shape[1]
    last = rows * half

    def around(d):
        piece = slice(d * half, (d + 1) * half)
        lower = near[0:rows, piece, :].reshape(last, lanes)
        upper = near[1 : rows + 1, piece, :].reshape(last, lanes)
        return [lower, upper]

    parts = []
    for d in range(4):
        parts += around(d)
    all_w = weights[...].reshape(4 * fine, fine)
    feature[...] = product(jnp.concatenate(parts, axis=1), all_w, 1, 0)
    for d in range(4):
        conv_acc[d] = product(act_t[...], jnp.concatenate(around(d), axis=1), 1, 0)
    at_north = lax.axis_index("lat") == 0
    at_south = lax.axis_index("lat") == lax.axis_size("lat") - 1
    north = pl.ds(pl.multiple_of(jnp.where(at_north, lanes, 0), lanes), lanes)
    south = pl.ds(pl.multiple_of(jnp.where(at_south, 0, lanes), lanes), lanes)
    shape = (half, lanes)
    total = [jnp.zeros(shape, F32), jnp.zeros(shape, F32)]
    for d in range(4):
        top = caps[0, d * half : (d + 1) * half, :]
        end = caps[1, d * half : (d + 1) * half, :]
        total[0] += product(top, weights[d, north, 0:lanes], 1, 0)
        total[1] += product(end, weights[d, south, lanes:fine], 1, 0)
        conv_acc[d, 0:lanes, north] += product(act_t[0:lanes, 0:half], top, 1, 0)
        padded = jnp.concatenate([jnp.zeros_like(end), end], axis=0)
        conv_acc[d, lanes:fine, south] += product(
            act_t[lanes:fine, last - 2 * half : last], padded, 1, 0
        )
    feature[0:half, 0:lanes] += total[0]
    feature[last - half : last, lanes:fine] += total[1]


def finish_kernel(x, feature, slope, conv_acc, act_rim, col_a, col_b, weights, up_w,
                  grad, sums, rims, rim_feature, rim_conv):
    rows = act_rim.shape[1]
    fine, lanes = weights.shape[1], rims.shape[2]
    channels = lanes // 2
    half = x.shape[0] // rows
    group = math.gcd(rows, 8)
    cells = group * half
    odd = lax.rem(lax.axis_index("lon"), 2) == 1
    at_north = lax.axis_index("lat") == 0
    at_south = lax.axis_index("lat") == lax.axis_size("lat") - 1
    from_a = col_a[...].astype(F32)
    from_b = col_b[...].astype(F32)
    rims[0] = jnp.where(odd, from_a, from_b)
    rims[1] = jnp.where(odd, from_b, from_a)
    row_id = lax.broadcasted_iota(jnp.int32, (rows, lanes), 0)
    lane_id = lax.broadcasted_iota(jnp.int32, (rows, lanes), 1)
    top_corner = jnp.logical_and(row_id == 0, lane_id < channels)
    end_corner = jnp.logical_and(row_id == rows - 1, lane_id >= channels)
    for side, d in ((0, 0), (1, 3)):
        lower, upper = rims[side, 0:rows, :], rims[side, 1 : rows + 1, :]
        lower = jnp.where(jnp.logical_and(top_corner, at_north), 0.0, lower)
        upper = jnp.where(jnp.logical_and(end_corner, at_south), 0.0, upper)
        ring = jnp.concatenate([lower, upper], axis=1).astype(BF16)
        rim_feature[side] = product(ring, weights[d], 1, 0)
        rim_conv[side] = product(act_rim[side].astype(BF16), ring, 0, 0)

    def corner(mask, offset, low, high, swap):
        for side, d in ((0, 0), (1, 3)):
            piece = jnp.where(mask, rims[side, offset : offset + rows, :], 0.0)
            blank = jnp.zeros_like(piece)
            parts = [blank, piece] if swap else [piece, blank]
            cap = jnp.concatenate(parts, axis=1).astype(BF16)
            rim_feature[side, :, low:high] += product(cap, weights[d, :, low:high], 1, 0)
            rim_conv[side, low:high, :] += product(
                act_rim[side, :, low:high].astype(BF16), cap, 0, 0
            )

    @pl.when(at_north)
    def _():
        corner(top_corner, 0, 0, lanes, True)

    @pl.when(at_south)
    def _():
        corner(end_corner, 1, lanes, fine, False)

    sub_id = lax.broadcasted_iota(jnp.int32, (group, 8, fine), 1)
    up_grad = None
    for s in range(rows // group):
        at = slice(s * cells, (s + 1) * cells)
        inner = feature[at, :].reshape(group, half, fine)
        west = rim_feature[0, s * group : (s + 1) * group, :][:, None, :]
        east = rim_feature[1, s * group : (s + 1) * group, :][:, None, :]
        whole = jnp.concatenate(
            [
                inner[:, 0:8] + jnp.where(sub_id == 0, west, 0.0),
                inner[:, 8 : half - 8],
                inner[:, half - 8 :] + jnp.where(sub_id == 7, east, 0.0),
            ],
            axis=1,
        ).reshape(cells, fine)
        pre = (whole * slope[at, :]).astype(BF16)
        grad[at, :] = product(pre, up_w[...], 1, 0).astype(BF16)
        term = product(pre, x[at, :], 0, 0)
        up_grad = term if up_grad is None else up_grad + term
    sums[0:fine, :] = up_grad.astype(BF16)

    def part(d, block):
        at = slice(block * channels, (block + 1) * channels)
        value = conv_acc[d, at, :]
        if d == 0:
            value = value + rim_conv[0, at, :]
        if d == 3:
            value = value + rim_conv[1, at, :]
        return value

    taps = []
    for b in (-1, 0, 1):
        upper = part(1 - b, 0) + part(2 - b, 1)
        lower = part(1 - b, 2) + part(2 - b, 3)
        taps.append(upper + pltpu.roll(lower, fine - channels, 1))
    turned = jnp.concatenate(taps[0:2], axis=0).T
    sums[fine : fine + 3 * channels, :] = turned[0 : 3 * channels].astype(BF16)
    turned = jnp.concatenate([taps[2], pltpu.roll(taps[2], fine - channels, 1)], axis=0).T
    sums[fine + 3 * channels : fine + 4 * channels, :] = turned[0:channels].astype(BF16)
    sums[fine + 4 * channels : fine + 5 * channels, :] = turned[2 * channels : 3 * channels].astype(BF16)


def unpack_kernel(whole, tconv_grad, conv_grad):
    fine, lanes = tconv_grad.shape
    channels = conv_grad.shape[0]
    tconv_grad[...] = whole[0:fine].astype(F32)
    block = [
        whole[fine + k * channels : fine + (k + 1) * channels].astype(F32) for k in range(5)
    ]
    singles = (block[4][:, :channels], block[3][:, channels:], block[3][:, :channels])
    for a in range(3):
        start = 3 * a * channels
        conv_grad[:, start : start + lanes] = block[2 - a]
        conv_grad[:, start + lanes : start + lanes + channels] = singles[a]


def summed_everywhere(part, scale):
    members = lax.axis_size(AXES)
    rows, lanes = part.shape
    piece = -(-rows // members)
    if members * piece > rows:
        part = jnp.pad(part, ((0, members * piece - rows), (0, 0)))
    parts = lax.all_to_all(part.reshape(members, piece, lanes), AXES, 0, 0, tiled=True)
    own = (jnp.sum(parts.astype(F32), axis=0) * scale).astype(part.dtype)
    spread = jnp.broadcast_to(own[None], (members, piece, lanes))
    whole = lax.all_to_all(spread, AXES, 0, 0, tiled=True)
    return whole.reshape(members * piece, lanes)[:rows]


def row_routes(lats, lons):
    half = lons // 2
    there = []
    for lat in range(lats):
        for lon in range(lons):
            if lon < half:
                target = (lat + 1, lon) if lat + 1 < lats else (lat, lon + half)
            else:
                target = (lat - 1, lon) if lat > 0 else (lat, lon - half)
            there.append((lat * lons + lon, target[0] * lons + target[1]))
    return there, [(b, a) for a, b in there]


def per_device(coarse_field, cotangent, tconv_weight, conv_weight):
    batch, channels, rows, cols = cotangent.shape
    in_channels = coarse_field.shape[1]
    lats, lons = lax.axis_size("lat"), lax.axis_size("lon")
    assert batch == 1 and lons % 2 == 0
    coarse_rows, half = rows // 2, cols // 2
    cells = coarse_rows * half
    pairs = coarse_rows + 1
    fine = 4 * channels
    lanes = 2 * channels
    scale = 1.0 / math.sqrt(batch * rows * cols * lats * lons)

    cot = cotangent.reshape(channels, rows, cols).transpose(1, 0, 2)
    x = coarse_field.transpose(0, 2, 3, 1).reshape(cells, in_channels)
    up_w = tconv_weight.reshape(fine, in_channels)

    first_half = lax.axis_index("lon") < lons // 2
    top, bottom = cot[0], cot[rows - 1]
    there, back = row_routes(lats, lons)
    row_a = lax.ppermute(jnp.where(first_half, bottom, top), AXES, there)
    row_b = lax.ppermute(jnp.where(first_half, top, bottom), AXES, back)

    slope, act_t, act_rim, weights = pl.pallas_call(
        up_kernel,
        out_shape=(
            pltpu.VMEM((cells, fine), F32),
            pltpu.VMEM((fine, cells), BF16),
            pltpu.VMEM((2, coarse_rows, fine), F32),
            pltpu.VMEM((4, fine, fine), BF16),
        ),
        in_specs=[VMEM] * 3,
        out_specs=(VMEM,) * 4,
        scratch_shapes=[pltpu.VMEM((2, channels, 10 * channels), BF16)],
        compiler_params=LIMIT,
        name="up",
    )(x, up_w, conv_weight)
    slope, act_t, act_rim, weights = map(resident, (slope, act_t, act_rim, weights))

    near, pick, edges = pl.pallas_call(
        gather_kernel,
        out_shape=(
            pltpu.VMEM((pairs, 4 * half, lanes), BF16),
            pltpu.VMEM((4 * half, cols), BF16),
            pltpu.VMEM((2, pairs, lanes), F32),
        ),
        in_specs=[VMEM] * 2,
        out_specs=(VMEM,) * 3,
        compiler_params=LIMIT,
        name="gather",
    )(resident(cot), act_rim)

    caps, send_a, send_b = pl.pallas_call(
        edge_kernel,
        out_shape=(
            pltpu.VMEM((2, 4 * half, lanes), BF16),
            pltpu.VMEM((pairs, lanes), BF16),
            pltpu.VMEM((pairs, lanes), BF16),
        ),
        in_specs=[VMEM] * 4,
        out_specs=(VMEM,) * 3,
        compiler_params=LIMIT,
        name="edge",
    )(resident(row_a), resident(row_b), resident(pick), resident(edges))

    inner = [(i, i ^ 1) for i in range(lons)]
    outer = [(i, (i + (1 if i % 2 else -1)) % lons) for i in range(lons)]
    col_a = lax.ppermute(send_a, "lon", inner)
    col_b = lax.ppermute(send_b, "lon", outer)

    feature, conv_acc = pl.pallas_call(
        spread_kernel,
        out_shape=(pltpu.VMEM((cells, fine), F32), pltpu.VMEM((4, fine, fine), F32)),
        in_specs=[VMEM] * 4,
        out_specs=(VMEM,) * 2,
        compiler_params=LIMIT,
        name="spread",
    )(resident(near), resident(caps), act_t, weights)

    grad, sums = pl.pallas_call(
        finish_kernel,
        out_shape=(
            jax.ShapeDtypeStruct((cells, in_channels), BF16),
            pltpu.VMEM((fine + 5 * channels, lanes), BF16),
        ),
        in_specs=[VMEM] * 9,
        out_specs=(VMEM,) * 2,
        scratch_shapes=[
            pltpu.VMEM((2, pairs, lanes), F32),
            pltpu.VMEM((2, coarse_rows, fine), F32),
            pltpu.VMEM((2, fine, fine), F32),
        ],
        compiler_params=LIMIT,
        name="finish",
    )(
        x, resident(feature), slope, resident(conv_acc), act_rim,
        resident(col_a), resident(col_b), weights, up_w,
    )

    whole = summed_everywhere(sums, scale)
    tconv_grad, conv_grad = pl.pallas_call(
        unpack_kernel,
        out_shape=(
            jax.ShapeDtypeStruct((fine, in_channels), F32),
            jax.ShapeDtypeStruct((channels, 9 * channels), F32),
        ),
        in_specs=[VMEM],
        out_specs=(VMEM,) * 2,
        compiler_params=LIMIT,
        name="unpack",
    )(resident(whole))
    tconv_grad = tconv_grad.reshape(4, channels, in_channels)
    coarse_grad = grad.reshape(1, coarse_rows, half, in_channels).transpose(0, 3, 1, 2)
    return (coarse_grad, tconv_grad, conv_grad)


def solution(mesh):
    return jax.shard_map(
        per_device,
        mesh=mesh,
        in_specs=(P(None, None, "lat", "lon"), P(None, None, "lat", "lon"), P(), P()),
        out_specs=(P(None, None, "lat", "lon"), P(), P()),
        check_vma=False,
    )
```

```python
import math

import jax
import jax.numpy as jnp
from jax import lax
from jax.experimental import pallas as pl
from jax.experimental.pallas import tpu as pltpu
from jax.sharding import PartitionSpec as P


F32, BF16 = jnp.float32, jnp.bfloat16
AXES = ("lat", "lon")
SHIFTS = (-1, 0, 1, 2)
VMEM = pl.BlockSpec(memory_space=pltpu.VMEM)
LIMIT = pltpu.CompilerParams(vmem_limit_bytes=24 * 2**20)


def product(lhs, rhs, lhs_dim, rhs_dim):
    dims = (((lhs_dim,), (rhs_dim,)), ((), ()))
    return lax.dot_general(lhs, rhs, dims, preferred_element_type=F32)


def resident(array):
    return pltpu.with_memory_space_constraint(array, pltpu.VMEM)


def place_weights(conv_w, weights, packed):
    channels, width = conv_w.shape
    pair = 2 * channels
    packed[0, :, 0:width] = conv_w[...]
    packed[1, :, 0 : width - channels] = conv_w[:, channels:width]
    weights[...] = jnp.zeros_like(weights)
    for e in range(4):
        for p in range(2):
            a = p - SHIFTS[e]
            if abs(a) > 1:
                continue
            tap = 3 * (a + 1)
            rows = slice(e * channels, (e + 1) * channels)
            low = p * pair
            for d in range(4):
                first = tap - SHIFTS[d] + 1
                if d == 0:
                    base = packed[first % 2, :, (first - first % 2) * channels :][:, 0:channels]
                    weights[d, rows, low : low + channels] = base
                elif d == 3:
                    weights[d, rows, low + channels : low + pair] = conv_w[
                        :, tap * channels : (tap + 1) * channels
                    ]
                else:
                    start = (first - first % 2) * channels
                    weights[d, rows, low : low + pair] = packed[
                        first % 2, :, start : start + pair
                    ]


def up_kernel(x, up_w, conv_w, slope, act_t, act_rim, weights, packed):
    rows = act_rim.shape[1]
    half = x.shape[0] // rows
    group = math.gcd(rows, 8)
    cells = group * half
    place_weights(conv_w, weights, packed)

    def step(s, carry):
        start = pl.multiple_of(s * cells, cells)
        up = product(x[pl.ds(start, cells), :], up_w[...], 1, 1)
        gate = 1.0 / (1.0 + jnp.exp(-up))
        active = up * gate
        slope[pl.ds(start, cells), :] = gate * (1.0 + up * (1.0 - gate))
        act_t[:, pl.ds(start, cells)] = active.astype(BF16).T
        for k in range(group):
            at = pl.ds(s * group + k, 1)
            act_rim[0, at, :] = active[k * half : k * half + 1]
            act_rim[1, at, :] = active[(k + 1) * half - 1 : (k + 1) * half]
        return carry

    lax.fori_loop(0, rows // group, step, 0, unroll=True)


def gather_kernel(cot, after, near, pick, edges):
    rows, channels, cols = cot.shape
    half = cols // 2
    pairs = near.shape[0]
    row_id = lax.broadcasted_iota(jnp.int32, (4 * half, cols), 0)
    col_id = lax.broadcasted_iota(jnp.int32, (4 * half, cols), 1)
    hit = col_id == 2 * (row_id % half) + row_id // half - 1
    pick[...] = jnp.where(hit, 1.0, 0.0).astype(BF16)

    def emit(m, block):
        near[m] = block.astype(BF16)
        edges[0, pl.ds(m, 1), :] = block[half : half + 1]
        edges[1, pl.ds(m, 1), :] = block[3 * half - 1 : 3 * half]

    def middle(q, carry):
        m = 1 + 2 * q
        four = cot[pl.ds(2 * m - 1, 4)].reshape(4 * channels, cols)
        out = product(pick[...], four, 1, 1)
        emit(m, out[:, : 2 * channels])
        emit(m + 1, out[:, 2 * channels :])
        return carry

    lax.fori_loop(0, (pairs - 3) // 2, middle, 0, unroll=5)
    blank = jnp.zeros((channels, cols), BF16)
    two = [blank, cot[0], cot[rows - 1], blank]
    out = product(pick[...], jnp.concatenate(two, axis=0), 1, 1)
    emit(0, out[:, : 2 * channels])
    emit(pairs - 1, out[:, 2 * channels :])
    m = pairs - 2
    emit(m, product(pick[...], cot[2 * m - 1 : 2 * m + 1].reshape(2 * channels, cols), 1, 1))


def edge_kernel(recv_a, recv_b, pick, edges, caps, send_a, send_b):
    quad = caps.shape[1]
    half, pairs = quad // 4, edges.shape[1]
    channels = recv_a.shape[0]
    first_half = 2 * lax.axis_index("lon") < lax.axis_size("lon")
    odd = lax.rem(lax.axis_index("lon"), 2) == 1
    from_a = recv_a[...].astype(F32)
    from_b = recv_b[...].astype(F32)
    blank = jnp.zeros((channels, recv_a.shape[1]), BF16)
    top = jnp.where(first_half, from_a, from_b).astype(BF16)
    bottom = jnp.where(first_half, from_b, from_a).astype(BF16)
    out = product(pick[...], jnp.concatenate([top, blank, blank, bottom], axis=0), 1, 1)
    lanes = 2 * channels
    for side in range(2):
        caps[side] = out[:, side * lanes : (side + 1) * lanes].astype(BF16)
    row_id = lax.broadcasted_iota(jnp.int32, (pairs, lanes), 0)
    rim = []
    for side, at in ((0, half), (1, 3 * half - 1)):
        line = out[at : at + 1]
        rim.append(
            edges[side]
            + jnp.where(row_id == 0, line[:, :lanes], 0.0)
            + jnp.where(row_id == pairs - 1, line[:, lanes:], 0.0)
        )
    send_a[...] = jnp.where(odd, rim[0], rim[1]).astype(BF16)
    send_b[...] = jnp.where(odd, rim[1], rim[0]).astype(BF16)


def spread_kernel(near, caps, act_t, weights, feature, conv_acc):
    pairs, quad, lanes = near.shape
    half, rows, fine = quad // 4, pairs - 1, weights.shape[1]
    last = rows * half

    def around(d):
        piece = slice(d * half, (d + 1) * half)
        lower = near[0:rows, piece, :].reshape(last, lanes)
        upper = near[1 : rows + 1, piece, :].reshape(last, lanes)
        return [lower, upper]

    parts = []
    for d in range(4):
        parts += around(d)
    all_w = weights[...].reshape(4 * fine, fine)
    feature[...] = product(jnp.concatenate(parts, axis=1), all_w, 1, 0)
    for d in range(4):
        conv_acc[d] = product(act_t[...], jnp.concatenate(around(d), axis=1), 1, 0)
    at_north = lax.axis_index("lat") == 0
    at_south = lax.axis_index("lat") == lax.axis_size("lat") - 1
    north = pl.ds(pl.multiple_of(jnp.where(at_north, lanes, 0), lanes), lanes)
    south = pl.ds(pl.multiple_of(jnp.where(at_south, 0, lanes), lanes), lanes)
    shape = (half, lanes)
    total = [jnp.zeros(shape, F32), jnp.zeros(shape, F32)]
    for d in range(4):
        top = caps[0, d * half : (d + 1) * half, :]
        end = caps[1, d * half : (d + 1) * half, :]
        total[0] += product(top, weights[d, north, 0:lanes], 1, 0)
        total[1] += product(end, weights[d, south, lanes:fine], 1, 0)
        conv_acc[d, 0:lanes, north] += product(act_t[0:lanes, 0:half], top, 1, 0)
        padded = jnp.concatenate([jnp.zeros_like(end), end], axis=0)
        conv_acc[d, lanes:fine, south] += product(
            act_t[lanes:fine, last - 2 * half : last], padded, 1, 0
        )
    feature[0:half, 0:lanes] += total[0]
    feature[last - half : last, lanes:fine] += total[1]


def finish_kernel(x, feature, slope, conv_acc, act_rim, col_a, col_b, weights, up_w,
                  grad_out, sums, rims, rim_feature, rim_conv, grad, sems):
    rows = act_rim.shape[1]
    fine, lanes = weights.shape[1], rims.shape[2]
    channels = lanes // 2
    half = x.shape[0] // rows
    group = math.gcd(rows, 16)
    cells = group * half
    odd = lax.rem(lax.axis_index("lon"), 2) == 1
    at_north = lax.axis_index("lat") == 0
    at_south = lax.axis_index("lat") == lax.axis_size("lat") - 1
    from_a = col_a[...].astype(F32)
    from_b = col_b[...].astype(F32)
    rims[0] = jnp.where(odd, from_a, from_b)
    rims[1] = jnp.where(odd, from_b, from_a)
    row_id = lax.broadcasted_iota(jnp.int32, (rows, lanes), 0)
    lane_id = lax.broadcasted_iota(jnp.int32, (rows, lanes), 1)
    top_corner = jnp.logical_and(row_id == 0, lane_id < channels)
    end_corner = jnp.logical_and(row_id == rows - 1, lane_id >= channels)
    for side, d in ((0, 0), (1, 3)):
        lower, upper = rims[side, 0:rows, :], rims[side, 1 : rows + 1, :]
        lower = jnp.where(jnp.logical_and(top_corner, at_north), 0.0, lower)
        upper = jnp.where(jnp.logical_and(end_corner, at_south), 0.0, upper)
        ring = jnp.concatenate([lower, upper], axis=1).astype(BF16)
        rim_feature[side] = product(ring, weights[d], 1, 0)
        rim_conv[side] = product(act_rim[side].astype(BF16), ring, 0, 0)

    def corner(mask, offset, low, high, swap):
        for side, d in ((0, 0), (1, 3)):
            piece = jnp.where(mask, rims[side, offset : offset + rows, :], 0.0)
            blank = jnp.zeros_like(piece)
            parts = [blank, piece] if swap else [piece, blank]
            cap = jnp.concatenate(parts, axis=1).astype(BF16)
            rim_feature[side, :, low:high] += product(cap, weights[d, :, low:high], 1, 0)
            rim_conv[side, low:high, :] += product(
                act_rim[side, :, low:high].astype(BF16), cap, 0, 0
            )

    @pl.when(at_north)
    def _():
        corner(top_corner, 0, 0, lanes, True)

    @pl.when(at_south)
    def _():
        corner(end_corner, 1, lanes, fine, False)

    sub_id = lax.broadcasted_iota(jnp.int32, (group, 8, fine), 1)
    up_grad = None
    saves = []
    for s in range(rows // group):
        at = slice(s * cells, (s + 1) * cells)
        inner = feature[at, :].reshape(group, half, fine)
        west = rim_feature[0, s * group : (s + 1) * group, :][:, None, :]
        east = rim_feature[1, s * group : (s + 1) * group, :][:, None, :]
        whole = jnp.concatenate(
            [
                inner[:, 0:8] + jnp.where(sub_id == 0, west, 0.0),
                inner[:, 8 : half - 8],
                inner[:, half - 8 :] + jnp.where(sub_id == 7, east, 0.0),
            ],
            axis=1,
        ).reshape(cells, fine)
        pre = (whole * slope[at, :]).astype(BF16)
        grad[at, :] = product(pre, up_w[...], 1, 0).astype(BF16)
        saves.append(pltpu.make_async_copy(grad.at[at], grad_out.at[at], sems.at[s]))
        saves[s].start()
        term = product(pre, x[at, :], 0, 0)
        up_grad = term if up_grad is None else up_grad + term
    sums[0:fine, :] = up_grad.astype(BF16)

    def part(d, block):
        at = slice(block * channels, (block + 1) * channels)
        value = conv_acc[d, at, :]
        if d == 0:
            value = value + rim_conv[0, at, :]
        if d == 3:
            value = value + rim_conv[1, at, :]
        return value

    taps = []
    for b in (-1, 0, 1):
        upper = part(1 - b, 0) + part(2 - b, 1)
        lower = part(1 - b, 2) + part(2 - b, 3)
        taps.append(upper + pltpu.roll(lower, fine - channels, 1))
    turned = jnp.concatenate(taps[0:2], axis=0).T
    sums[fine : fine + 3 * channels, :] = turned[0 : 3 * channels].astype(BF16)
    turned = jnp.concatenate([taps[2], pltpu.roll(taps[2], fine - channels, 1)], axis=0).T
    sums[fine + 3 * channels : fine + 4 * channels, :] = turned[0:channels].astype(BF16)
    sums[fine + 4 * channels : fine + 5 * channels, :] = turned[2 * channels : 3 * channels].astype(BF16)
    for save in saves:
        save.wait()


def unpack_kernel(whole, tconv_grad, conv_grad):
    fine, lanes = tconv_grad.shape
    channels = conv_grad.shape[0]
    tconv_grad[...] = whole[0:fine].astype(F32)
    block = [
        whole[fine + k * channels : fine + (k + 1) * channels].astype(F32) for k in range(5)
    ]
    singles = (block[4][:, :channels], block[3][:, channels:], block[3][:, :channels])
    for a in range(3):
        start = 3 * a * channels
        conv_grad[:, start : start + lanes] = block[2 - a]
        conv_grad[:, start + lanes : start + lanes + channels] = singles[a]


def summed_everywhere(part, scale):
    members = lax.axis_size(AXES)
    rows, lanes = part.shape
    piece = -(-rows // members)
    if members * piece > rows:
        part = jnp.pad(part, ((0, members * piece - rows), (0, 0)))
    parts = lax.all_to_all(part.reshape(members, piece, lanes), AXES, 0, 0, tiled=True)
    own = (jnp.sum(parts.astype(F32), axis=0) * scale).astype(part.dtype)
    spread = jnp.broadcast_to(own[None], (members, piece, lanes))
    whole = lax.all_to_all(spread, AXES, 0, 0, tiled=True)
    return whole.reshape(members * piece, lanes)[:rows]


def row_routes(lats, lons):
    half = lons // 2
    there = []
    for lat in range(lats):
        for lon in range(lons):
            if lon < half:
                target = (lat + 1, lon) if lat + 1 < lats else (lat, lon + half)
            else:
                target = (lat - 1, lon) if lat > 0 else (lat, lon - half)
            there.append((lat * lons + lon, target[0] * lons + target[1]))
    return there, [(b, a) for a, b in there]


def per_device(coarse_field, cotangent, tconv_weight, conv_weight):
    batch, channels, rows, cols = cotangent.shape
    in_channels = coarse_field.shape[1]
    lats, lons = lax.axis_size("lat"), lax.axis_size("lon")
    assert batch == 1 and lons % 2 == 0
    coarse_rows, half = rows // 2, cols // 2
    cells = coarse_rows * half
    pairs = coarse_rows + 1
    fine = 4 * channels
    lanes = 2 * channels
    scale = 1.0 / math.sqrt(batch * rows * cols * lats * lons)

    cot = cotangent.reshape(channels, rows, cols).transpose(1, 0, 2)
    x = coarse_field.transpose(0, 2, 3, 1).reshape(cells, in_channels)
    up_w = tconv_weight.reshape(fine, in_channels)

    first_half = lax.axis_index("lon") < lons // 2
    top, bottom = cot[0], cot[rows - 1]
    there, back = row_routes(lats, lons)
    row_a = lax.ppermute(jnp.where(first_half, bottom, top), AXES, there)
    row_b = lax.ppermute(jnp.where(first_half, top, bottom), AXES, back)

    slope, act_t, act_rim, weights = pl.pallas_call(
        up_kernel,
        out_shape=(
            pltpu.VMEM((cells, fine), F32),
            pltpu.VMEM((fine, cells), BF16),
            pltpu.VMEM((2, coarse_rows, fine), F32),
            pltpu.VMEM((4, fine, fine), BF16),
        ),
        in_specs=[VMEM] * 3,
        out_specs=(VMEM,) * 4,
        scratch_shapes=[pltpu.VMEM((2, channels, 10 * channels), BF16)],
        compiler_params=LIMIT,
        name="up",
    )(x, up_w, conv_weight)
    slope, act_t, act_rim, weights = map(resident, (slope, act_t, act_rim, weights))

    near, pick, edges = pl.pallas_call(
        gather_kernel,
        out_shape=(
            pltpu.VMEM((pairs, 4 * half, lanes), BF16),
            pltpu.VMEM((4 * half, cols), BF16),
            pltpu.VMEM((2, pairs, lanes), F32),
        ),
        in_specs=[VMEM] * 2,
        out_specs=(VMEM,) * 3,
        compiler_params=LIMIT,
        name="gather",
    )(resident(cot), act_rim)

    caps, send_a, send_b = pl.pallas_call(
        edge_kernel,
        out_shape=(
            pltpu.VMEM((2, 4 * half, lanes), BF16),
            pltpu.VMEM((pairs, lanes), BF16),
            pltpu.VMEM((pairs, lanes), BF16),
        ),
        in_specs=[VMEM] * 4,
        out_specs=(VMEM,) * 3,
        compiler_params=LIMIT,
        name="edge",
    )(resident(row_a), resident(row_b), resident(pick), resident(edges))

    inner = [(i, i ^ 1) for i in range(lons)]
    outer = [(i, (i + (1 if i % 2 else -1)) % lons) for i in range(lons)]
    col_a = lax.ppermute(send_a, "lon", inner)
    col_b = lax.ppermute(send_b, "lon", outer)

    feature, conv_acc = pl.pallas_call(
        spread_kernel,
        out_shape=(pltpu.VMEM((cells, fine), F32), pltpu.VMEM((4, fine, fine), F32)),
        in_specs=[VMEM] * 4,
        out_specs=(VMEM,) * 2,
        compiler_params=LIMIT,
        name="spread",
    )(resident(near), resident(caps), act_t, weights)

    grad, sums = pl.pallas_call(
        finish_kernel,
        out_shape=(
            jax.ShapeDtypeStruct((cells, in_channels), BF16),
            pltpu.VMEM((fine + 5 * channels, lanes), BF16),
        ),
        in_specs=[VMEM] * 9,
        out_specs=(pl.BlockSpec(memory_space=pltpu.HBM), VMEM),
        scratch_shapes=[
            pltpu.VMEM((2, pairs, lanes), F32),
            pltpu.VMEM((2, coarse_rows, fine), F32),
            pltpu.VMEM((2, fine, fine), F32),
            pltpu.VMEM((cells, in_channels), BF16),
            pltpu.SemaphoreType.DMA((coarse_rows // math.gcd(coarse_rows, 16),)),
        ],
        compiler_params=LIMIT,
        name="finish",
    )(
        x, resident(feature), slope, resident(conv_acc), act_rim,
        resident(col_a), resident(col_b), weights, up_w,
    )

    whole = summed_everywhere(sums, scale)
    tconv_grad, conv_grad = pl.pallas_call(
        unpack_kernel,
        out_shape=(
            jax.ShapeDtypeStruct((fine, in_channels), F32),
            jax.ShapeDtypeStruct((channels, 9 * channels), F32),
        ),
        in_specs=[VMEM],
        out_specs=(VMEM,) * 2,
        compiler_params=LIMIT,
        name="unpack",
    )(resident(whole))
    tconv_grad = tconv_grad.reshape(4, channels, in_channels)
    coarse_grad = grad.reshape(1, coarse_rows, half, in_channels).transpose(0, 3, 1, 2)
    return (coarse_grad, tconv_grad, conv_grad)


def solution(mesh):
    return jax.shard_map(
        per_device,
        mesh=mesh,
        in_specs=(P(None, None, "lat", "lon"), P(None, None, "lat", "lon"), P(), P()),
        out_specs=(P(None, None, "lat", "lon"), P(), P()),
        check_vma=False,
    )
```
